32 devices in a mesh: seq: 8 (over z, x), tensor: 4 (over y, core).
Axes of the slice: x: 2, y: 2, z: 4, core: 2. Of those that a mesh axis runs over, the one named last changes fastest.
Arguments:
- hidden: bfloat16 [2048, 53248], P('seq', 'tensor'), may hold values from -6 to 6
- grad_out: bfloat16 [2048, 16384], P('seq', 'tensor'), may hold values from -0.13183594 to 0.13183594
- block_rows: int32 [4, 24], P('tensor'), may hold values from 0 to 103
- block_cols: int32 [4, 24], P('tensor'), may hold values from 0 to 127, as said below
- block_owner: int32 [4, 24], P('tensor'), may hold values from 0 to 7, never falling along the last dimension, each value on 1 to 8 neighbouring positions
Outputs:
- block_grads: bfloat16 [4, 64, 128, 128], P('tensor', 'seq')
The draws below stay inside these ranges and needn't reach their ends.
Inputs may be any that keep to these rules, and one draw needn't show every extreme that they name: Every row of block_owner never falls along the list; each owner holds 1 to 8 blocks of a row, and some owner holds exactly 8. Each row of block_cols names exactly 6 distinct values among each run of 128 // 4 values that starts at a multiple of it.
All inputs are finite; a program needn't handle non-finite values.
Results may differ from the reference program's by a relative error of at most 0.0085.
Values may be sent and summed in bfloat16 or wider, within the bound.
No kernel may reach another device: no remote copies, remote signals or barrier semaphores. Data moves between devices by JAX's collectives and lax.ppermute only.
A program may use at most 128 MiB of HBM per device.

```python
import math
import jax
import jax.numpy as jnp
import numpy as np
from jax import lax

D = 16384
FF = 53248
TOK_DEV = 256
BLOCK = 128
CAP = 8
TOKENS = 2048
NBT = 24
RB = 104
CB = 128
UCOL = 6
N_SEQ = 8
N_TENSOR = 4


def draw_block_cols(key, part):
    key_pick, key_fill, key_order = jax.random.split(jax.random.fold_in(key, 7), 3)
    per_peer = CB // N_TENSOR
    scores = jax.random.randint(key_pick, (N_TENSOR, N_TENSOR, per_peer), 0, 1 << 20)
    scores = scores * per_peer + jnp.arange(per_peer, dtype=jnp.int32)[None, None, :]
    ranked = jnp.argsort(scores, axis=2).astype(jnp.int32)[:, :, :UCOL]
    chosen = ranked + (jnp.arange(N_TENSOR, dtype=jnp.int32) * per_peer)[None, :, None]
    chosen = chosen.reshape(N_TENSOR, N_TENSOR * UCOL)
    fill_ids = jax.random.randint(key_fill, (N_TENSOR, NBT - N_TENSOR * UCOL), 0, N_TENSOR * UCOL)
    filled = jnp.take_along_axis(chosen, fill_ids, axis=1)
    columns = jnp.concatenate([chosen, filled], axis=1)
    order_keys = jax.random.randint(key_order, (N_TENSOR, NBT), 0, 1 << 20)
    order_keys = order_keys * NBT + jnp.arange(NBT, dtype=jnp.int32)[None, :]
    order = jnp.argsort(order_keys, axis=1).astype(jnp.int32)
    return jnp.take_along_axis(columns, order, axis=1).astype(jnp.int32)


def touch_ends(array, rng, smallest, top_value):
    spot = [jax.random.randint(jax.random.fold_in(rng, axis), (), 0, length) for axis, length in enumerate(array.shape)]
    widest = array.shape.index(max(array.shape))
    neighbour = spot[:widest] + [(spot[widest] + 1) % array.shape[widest]] + spot[widest + 1:]
    return array.at[tuple(spot)].set(smallest).at[tuple(neighbour)].set(top_value)


def block_scale(own_key, extent, cuts, smallest, top_value):
    loudness = 1.0
    for dim, blocks in cuts:
        heights = jax.random.uniform(jax.random.fold_in(jax.random.fold_in(own_key, 6), dim), (blocks,), jnp.float32, smallest / len(cuts), top_value / len(cuts))
        loudness = loudness * jnp.repeat(jnp.exp(heights), extent[dim] // blocks).reshape((-1,) + (1,) * (len(extent) - 1 - dim))
    return loudness


def cumulative_ranks(number_of, skew):
    weights = [(1 << 20) // math.isqrt(standing ** skew) + 1 for standing in range(1, number_of + 1)]
    spread = 1 + sum(weights) // (1 << 30)
    return np.cumsum(np.array([max(1, weight // spread) for weight in weights]))


def ranked_ids(stream_key, extent, amount, slope):
    grid = cumulative_ranks(amount, slope)
    ticket = jax.random.randint(jax.random.fold_in(stream_key, 1), extent, 0, int(grid[amount - 1]))
    standing = jnp.searchsorted(jnp.asarray(grid, jnp.int32), ticket, side="right")
    return jax.random.permutation(jax.random.fold_in(stream_key, 2), amount)[standing].astype(jnp.int32)


def split_up(number_of, total, most, lean):
    portions = [(1 << 20) // math.isqrt(standing ** lean) + 1 for standing in range(2, number_of + 1)]
    spare, given = total - most - (number_of - 1), [1] * (number_of - 1)
    while spare > 0:
        candidates = [i for i in range(number_of - 1) if given[i] < most]
        pool, remaining = sum([portions[i] for i in candidates]), spare
        for i in candidates:
            more = min(most - given[i], max(1, remaining * portions[i] // pool), spare)
            given[i] = given[i] + more
            spare = spare - more
    return np.array([most] + given)


def ragged_sizes(stream_key, amount, total, bound, skew):
    if amount == 2:
        one = jax.random.randint(stream_key, (), max(1, total - bound), min(bound, total - 1) + 1)
        return jnp.stack([one, total - one])
    tallies = jnp.asarray(split_up(amount, total, bound, skew), jnp.int32)
    twos = (amount - 1) // 2
    donor, receiver = tallies[1:1 + 2 * twos:2], tallies[2:2 + 2 * twos:2]
    margin = jnp.minimum(donor - 1, bound - receiver)
    moved = jax.random.randint(jax.random.fold_in(stream_key, 1), (twos,), 0, 1 << 20) % (margin + 1)
    tallies = tallies.at[1:1 + 2 * twos:2].set(donor - moved).at[2:2 + 2 * twos:2].set(receiver + moved)
    return tallies[jax.random.permutation(jax.random.fold_in(stream_key, 2), amount)]


def bell_draw(key, shape, scale, limit, cuts=(), held_as=jnp.bfloat16):
    result = jax.random.normal(key, shape, jnp.float32) * scale
    if len(cuts) > 0:
        result = block_scale(key, shape, cuts, -0.22, 0.18) * result
    return jnp.clip(result, min=-limit, max=limit).astype(held_as)


def setup_inputs(seed: int = 0) -> dict:
    seeds = jax.random.split(jax.random.key(seed), 6)
    hidden = bell_draw(seeds[0], (TOKENS, FF), 1.0, 6.0, ((0, 8), (1, 4)))
    grad_out = bell_draw(seeds[1], (TOKENS, D), (TOKENS ** -0.5), 0.13183594, ((0, 8), (1, 4)))
    block_rows = touch_ends(ranked_ids(seeds[2], (N_TENSOR, NBT), RB, 2), jax.random.fold_in(seeds[2], 3), 0, RB - 1).astype(jnp.int32)
    block_cols = draw_block_cols(jax.random.fold_in(seeds[5], 71), 0)
    block_owner = jax.vmap(lambda own: jnp.searchsorted(jnp.cumsum(ragged_sizes(own, N_SEQ, NBT, CAP, 2)), jnp.arange(NBT), side="right"))(jax.random.split(seeds[4], N_TENSOR)).reshape((N_TENSOR, NBT)).astype(jnp.int32)
    return dict(hidden=hidden, grad_out=grad_out, block_rows=block_rows, block_cols=block_cols, block_owner=block_owner)


def reference(hidden, grad_out, block_rows, block_cols, block_owner):
    hidden_groups = hidden.reshape(TOKENS, N_TENSOR, RB, BLOCK).transpose(1, 0, 2, 3)
    grad_blocks = grad_out.reshape(TOKENS, CB, BLOCK)

    def one_group(inputs):
        hidden_group, row_ids, col_ids, owners = inputs
        hidden_sel = jnp.take(hidden_group, row_ids, axis=1).reshape(N_SEQ, TOK_DEV, NBT, BLOCK)
        grad_sel = jnp.take(grad_blocks, col_ids, axis=1).reshape(N_SEQ, TOK_DEV, NBT, BLOCK)
        partial_value = jnp.einsum("stkr,stkc->skrc", hidden_sel.astype(jnp.float32), grad_sel.astype(jnp.float32))
        partial_value = partial_value.astype(jnp.bfloat16)
        summed = jnp.sum(partial_value.astype(jnp.float32), axis=0).astype(jnp.bfloat16)
        members = (owners[None, :] == jnp.arange(N_SEQ, dtype=jnp.int32)[:, None]).astype(jnp.int32)
        counts = jnp.sum(members, axis=1)
        starts = jnp.cumsum(counts) - counts
        slot_ids = starts[:, None] + jnp.arange(CAP, dtype=jnp.int32)[None, :]
        is_live = jnp.arange(CAP, dtype=jnp.int32)[None, :] < counts[:, None]
        picked = jnp.take(summed, jnp.minimum(slot_ids, NBT - 1).reshape(-1).astype(jnp.int32), axis=0)
        picked = picked.reshape(N_SEQ, CAP, BLOCK, BLOCK)
        picked = jnp.where(is_live[:, :, None, None], picked, jnp.zeros_like(picked))
        return picked.reshape(N_SEQ * CAP, BLOCK, BLOCK)

    return lax.map(one_group, (hidden_groups, block_rows, block_cols, block_owner))
```

```python
import functools

import jax
import jax.numpy as jnp
from jax import lax
from jax.experimental import pallas as pl
from jax.experimental.pallas import tpu as pltpu
from jax.sharding import PartitionSpec as P

BLOCK = 128
CAP = 8
ROW_TILE = 16

SMEM = pl.BlockSpec(memory_space=pltpu.SMEM)
ANY = pl.BlockSpec(memory_space=pl.ANY)
VMEM = pl.BlockSpec(memory_space=pltpu.VMEM)


def pick_slots(summed, starts, counts):
    slot_ids = starts[:, None] + jnp.arange(CAP, dtype=jnp.int32)[None, :]
    is_live = jnp.arange(CAP, dtype=jnp.int32)[None, :] < counts[:, None]
    picked = jnp.take(summed, jnp.minimum(slot_ids, summed.shape[0] - 1).reshape(-1), axis=0)
    picked = picked.reshape(slot_ids.shape[0], CAP, BLOCK, BLOCK)
    return jnp.where(is_live[:, :, None, None], picked, jnp.zeros_like(picked))


def dense_on_device(hidden, grad_out, block_rows, block_cols, block_owner):
    tok_rows = hidden.shape[0]
    hidden_sel = jnp.take(hidden.reshape(tok_rows, -1, BLOCK), block_rows[0], axis=1)
    cotangent = lax.all_gather(grad_out, "tensor", axis=1, tiled=True)
    grad_sel = jnp.take(cotangent.reshape(tok_rows, -1, BLOCK), block_cols[0], axis=1)
    partial_value = jnp.einsum(
        "tkr,tkc->krc", hidden_sel, grad_sel, preferred_element_type=jnp.float32
    ).astype(jnp.bfloat16)
    seq_count = lax.axis_size("seq")
    members = (block_owner[0][None, :] == jnp.arange(seq_count, dtype=jnp.int32)[:, None]).astype(jnp.int32)
    counts = jnp.sum(members, axis=1)
    starts = jnp.cumsum(counts) - counts
    outgoing = pick_slots(partial_value, starts, counts)
    received = lax.all_to_all(outgoing, "seq", split_axis=0, concat_axis=0, tiled=True)
    return jnp.sum(received, axis=0, dtype=jnp.float32).astype(jnp.bfloat16)[None]


def column(ref, index):
    return ref.at[:, pl.ds(pl.multiple_of(index * BLOCK, BLOCK), BLOCK)]


def own_columns(table, cols, me, cols_per, per_peer):
    for j in range(per_peer):
        table[j] = 0

    def visit(k, found):
        local = cols[0, k] - me * cols_per
        hit = jnp.logical_and(local >= 0, local < cols_per)
        table[jnp.where(hit, jnp.minimum(found, per_peer - 1), per_peer)] = local
        return found + hit.astype(jnp.int32)

    lax.fori_loop(0, cols.shape[1], visit, jnp.int32(0), unroll=True)


def pack_kernel(peers, cols_per, per_peer, *refs):
    lists, grad_out, packed, (table, sems) = refs[:peers], refs[peers], refs[peers + 1 : 2 * peers + 1], refs[2 * peers + 1 :]
    me = lax.axis_index("tensor")
    copies = []
    for n in range(peers):
        own_columns(table, lists[n], me, cols_per, per_peer)
        for j in range(per_peer):
            copy = pltpu.make_async_copy(column(grad_out, table[j]), packed[n].at[j], sems.at[n, j])
            copy.start()
            copies.append(copy)
    for copy in copies:
        copy.wait()


def pack_for(lists, grad_out, per_peer):
    tok_rows, width = grad_out.shape
    peers = len(lists)
    return pl.pallas_call(
        functools.partial(pack_kernel, peers, width // BLOCK, per_peer),
        out_shape=[jax.ShapeDtypeStruct((per_peer, tok_rows, BLOCK), grad_out.dtype)] * peers,
        in_specs=[SMEM] * peers + [ANY],
        out_specs=[VMEM] * peers,
        scratch_shapes=[pltpu.SMEM((per_peer + 1,), jnp.int32), pltpu.SemaphoreType.DMA((peers, per_peer))],
        name="pack_columns",
    )(*lists, grad_out)


def multiply(pieces, left, right):
    product = lax.dot_general(left, right, (((0,), (0,)), ((), ())), preferred_element_type=jnp.float32)
    return product.astype(jnp.bfloat16).reshape(pieces, BLOCK // pieces, BLOCK)


def near_kernel(cols_per, per_peer, pieces, rows, cols, hidden, grad_out, arrived, out, hidden_far, hidden_near, grad_near, row_of, col_of, seen, sems):
    me = lax.axis_index("tensor")
    items = row_of.shape[0]
    for index in range(items // per_peer):
        seen[index] = 0
    for item in range(items):
        row_of[item] = 0
        col_of[item] = 0

    def visit(k, carry):
        col = cols[0, k]
        distance = (col // cols_per) ^ me
        rank = seen[distance]
        seen[distance] = rank + 1
        item = distance * per_peer + jnp.minimum(rank, per_peer - 1)
        row_of[item] = rows[0, k]
        col_of[item] = col % cols_per
        return carry

    lax.fori_loop(0, items, visit, 0, unroll=True)
    near = 2 * per_peer
    hidden_copies, grad_copies = [], []
    for item in range(items):
        there = hidden_near.at[item] if item < near else hidden_far.at[item - near]
        hidden_copies.append(pltpu.make_async_copy(column(hidden, row_of[item]), there, sems.at[0, item]))
        hidden_copies[-1].start()
        if item < per_peer:
            grad_copies.append(pltpu.make_async_copy(column(grad_out, col_of[item]), grad_near.at[item], sems.at[1, item]))
            grad_copies[-1].start()
    for item in range(near):
        hidden_copies[item].wait()
        if item < per_peer:
            grad_copies[item].wait()
        right = grad_near[item] if item < per_peer else arrived[item - per_peer]
        out[:, item] = multiply(pieces, hidden_near[item], right)
    for copy in hidden_copies[near:]:
        copy.wait()


def near_products(rows, cols, hidden, grad_out, arrived, per_peer, pieces):
    tok_rows, width = grad_out.shape
    items, near = cols.shape[1], 2 * per_peer
    return pl.pallas_call(
        functools.partial(near_kernel, width // BLOCK, per_peer, pieces),
        out_shape=[
            jax.ShapeDtypeStruct((pieces, near, BLOCK // pieces, BLOCK), jnp.bfloat16),
            jax.ShapeDtypeStruct((items - near, tok_rows, BLOCK), jnp.bfloat16),
        ],
        in_specs=[SMEM, SMEM, ANY, ANY, VMEM],
        out_specs=[VMEM, VMEM],
        scratch_shapes=[
            pltpu.VMEM((near, tok_rows, BLOCK), jnp.bfloat16),
            pltpu.VMEM((per_peer, tok_rows, BLOCK), jnp.bfloat16),
            pltpu.SMEM((items,), jnp.int32),
            pltpu.SMEM((items,), jnp.int32),
            pltpu.SMEM((items // per_peer,), jnp.int32),
            pltpu.SemaphoreType.DMA((2, items)),
        ],
        name="near_products",
    )(rows, cols, hidden, grad_out, arrived)


def far_kernel(first, pieces, hidden_far, arrived, out):
    for item in range(arrived.shape[0]):
        out[:, item] = multiply(pieces, hidden_far[first + item], arrived[item])


def far_products(first, hidden_far, arrived, pieces):
    return pl.pallas_call(
        functools.partial(far_kernel, first, pieces),
        out_shape=jax.ShapeDtypeStruct((pieces, arrived.shape[0], BLOCK // pieces, BLOCK), jnp.bfloat16),
        in_specs=[VMEM, VMEM],
        out_specs=VMEM,
        name="far_products",
    )(hidden_far, arrived)


def settle_kernel(cols_per, per_peer, cols, owners, *refs):
    received, (out, summed, seen) = refs[:-3], refs[-3:]
    base = 0
    for part in received:
        count = part.shape[1]
        summed[pl.ds(base, count)] = jnp.sum(part[...].astype(jnp.float32), axis=0).astype(jnp.bfloat16)
        base += count
    out[...] = jnp.zeros_like(out)
    me = lax.axis_index("tensor")
    for index in range(base // per_peer):
        seen[index] = 0

    def visit(k, carry):
        last_owner, last_slot = carry
        distance = (cols[0, k] // cols_per) ^ me
        rank = seen[distance]
        seen[distance] = rank + 1
        owner = owners[0, k]
        slot = jnp.where(owner == last_owner, last_slot + 1, 0)
        out[owner, jnp.minimum(slot, CAP - 1)] = summed[distance * per_peer + jnp.minimum(rank, per_peer - 1)]
        return owner, slot

    lax.fori_loop(0, cols.shape[1], visit, (jnp.int32(-1), jnp.int32(0)))


def settle(cols, owners, received, cols_per, per_peer):
    pieces, _, rows, _ = received[0].shape
    items = sum(part.shape[1] for part in received)
    return pl.pallas_call(
        functools.partial(settle_kernel, cols_per, per_peer),
        out_shape=jax.ShapeDtypeStruct((pieces, CAP, rows, BLOCK), jnp.bfloat16),
        in_specs=[SMEM, SMEM] + [VMEM] * len(received),
        out_specs=VMEM,
        scratch_shapes=[
            pltpu.VMEM((items, rows, BLOCK), jnp.bfloat16),
            pltpu.SMEM((items // per_peer,), jnp.int32),
        ],
        name="settle",
    )(cols, owners, *received)


def sparse_on_device(hidden, grad_out, block_rows, block_cols, block_owner):
    tensor_count, seq_count = lax.axis_size("tensor"), lax.axis_size("seq")
    cols_per = grad_out.shape[1] // BLOCK
    per_peer = block_cols.shape[1] // tensor_count

    def to_peer(value, distance):
        return lax.ppermute(value, "tensor", [(i, i ^ distance) for i in range(tensor_count)])

    def scatter(value):
        return lax.all_to_all(value, "seq", split_axis=0, concat_axis=0, tiled=True)

    peers = range(1, tensor_count)
    packed = pack_for([to_peer(block_cols, distance) for distance in peers], grad_out, per_peer)
    arrived = [to_peer(blocks, distance) for distance, blocks in zip(peers, packed)]
    near, hidden_far = near_products(block_rows, block_cols, hidden, grad_out, arrived[0], per_peer, seq_count)
    received = [scatter(near)]
    for n, blocks in enumerate(arrived[1:]):
        received.append(scatter(far_products(n * per_peer, hidden_far, blocks, seq_count)))
    placed = scatter(settle(block_cols, block_owner, received, cols_per, per_peer))
    return placed.transpose(1, 0, 2, 3).reshape(1, CAP, BLOCK, BLOCK)


def solution(mesh):
    tensor_count, seq_count = mesh.shape["tensor"], mesh.shape["seq"]
    placed = (
        P("seq", "tensor"),
        P("seq", "tensor"),
        P("tensor", None),
        P("tensor", None),
        P("tensor", None),
    )

    def on_device(hidden, grad_out, block_rows, block_cols, block_owner):
        listed = block_cols.shape[1]
        each_named_once = listed == 24 and tensor_count == 4
        whole_tiles = BLOCK % (seq_count * ROW_TILE) == 0
        step = sparse_on_device if each_named_once and whole_tiles else dense_on_device
        return step(hidden, grad_out, block_rows, block_cols, block_owner)

    return jax.shard_map(
        on_device,
        mesh=mesh,
        in_specs=placed,
        out_specs=P("tensor", "seq", None, None),
        check_vma=False,
    )
```

```python
import functools

import jax
import jax.numpy as jnp
from jax import lax
from jax.experimental import pallas as pl
from jax.experimental.pallas import tpu as pltpu
from jax.sharding import PartitionSpec as P


BLOCK = 128
CAP = 8
ROW_TILE = 16

SMEM = pl.BlockSpec(memory_space=pltpu.SMEM)
HBM = pl.BlockSpec(memory_space=pltpu.HBM)
VMEM = pl.BlockSpec(memory_space=pltpu.VMEM)


def pick_slots(summed, starts, counts):
    slot_ids = starts[:, None] + jnp.arange(CAP, dtype=jnp.int32)[None, :]
    is_live = jnp.arange(CAP, dtype=jnp.int32)[None, :] < counts[:, None]
    picked = jnp.take(summed, jnp.minimum(slot_ids, summed.shape[0] - 1).reshape(-1), axis=0)
    picked = picked.reshape(slot_ids.shape[0], CAP, BLOCK, BLOCK)
    return jnp.where(is_live[:, :, None, None], picked, jnp.zeros_like(picked))


def dense_on_device(hidden, grad_out, block_rows, block_cols, block_owner):
    tok_rows = hidden.shape[0]
    hidden_sel = jnp.take(hidden.reshape(tok_rows, -1, BLOCK), block_rows[0], axis=1)
    cotangent = lax.all_gather(grad_out, "tensor", axis=1, tiled=True)
    grad_sel = jnp.take(cotangent.reshape(tok_rows, -1, BLOCK), block_cols[0], axis=1)
    partial_value = jnp.einsum(
        "tkr,tkc->krc", hidden_sel, grad_sel, preferred_element_type=jnp.float32
    ).astype(jnp.bfloat16)
    seq_count = lax.axis_size("seq")
    members = (block_owner[0][None, :] == jnp.arange(seq_count, dtype=jnp.int32)[:, None]).astype(jnp.int32)
    counts = jnp.sum(members, axis=1)
    starts = jnp.cumsum(counts) - counts
    outgoing = pick_slots(partial_value, starts, counts)
    received = lax.all_to_all(outgoing, "seq", split_axis=0, concat_axis=0, tiled=True)
    return jnp.sum(received, axis=0, dtype=jnp.float32).astype(jnp.bfloat16)[None]


def scalars(value):
    return pltpu.with_memory_space_constraint(value, pltpu.SMEM)


def vectors(value):
    return pltpu.with_memory_space_constraint(value, pltpu.VMEM)


def column(ref, index):
    return ref.at[:, pl.ds(pl.multiple_of(index * BLOCK, BLOCK), BLOCK)]


def listed_at(table, cols, values, owner, cols_per, per_peer):
    for j in range(per_peer):
        table[j] = 0

    def visit(k, found):
        local = cols[0, k] - owner * cols_per
        hit = jnp.logical_and(local >= 0, local < cols_per)
        value = local if values is None else values[0, k]
        table[jnp.where(hit, jnp.minimum(found, per_peer - 1), per_peer)] = value
        return found + hit.astype(jnp.int32)

    lax.fori_loop(0, cols.shape[1], visit, jnp.int32(0), unroll=True)


def split_pieces(parts, kept, sent):
    me = lax.axis_index("seq")
    half = kept.shape[0]
    width = half.bit_length() - 1
    for index in range(half):
        apart = sum(((index >> (width - 1 - bit)) & 1) << (bit + 1) for bit in range(width))
        kept[index] = parts[me ^ apart]
        sent[index] = parts[me ^ apart ^ 1].astype(jnp.bfloat16)


def halve_kernel(kept, received, still, sent):
    half = still.shape[0]
    still[...] = kept[:half] + received[:half].astype(jnp.float32)
    sent[...] = (kept[half:] + received[half:].astype(jnp.float32)).astype(jnp.bfloat16)


def halve(kept, received):
    shape = (kept.shape[0] // 2,) + kept.shape[1:]
    return pl.pallas_call(
        halve_kernel,
        out_shape=[pltpu.VMEM(shape, jnp.float32), pltpu.VMEM(shape, jnp.bfloat16)],
        in_specs=[VMEM, VMEM],
        out_specs=[VMEM, VMEM],
    )(vectors(kept), vectors(received))


def finish_kernel(kept, received, out):
    out[...] = (kept[0] + received[0].astype(jnp.float32)).astype(jnp.bfloat16)


def finish(kept, received):
    return pl.pallas_call(
        finish_kernel, out_shape=pltpu.VMEM(kept.shape[1:], jnp.bfloat16), in_specs=[VMEM, VMEM], out_specs=VMEM
    )(vectors(kept), vectors(received))


def halved_shapes(pieces, items):
    shape = (pieces // 2, items, BLOCK // pieces, BLOCK)
    return [pltpu.VMEM(shape, jnp.float32), pltpu.VMEM(shape, jnp.bfloat16)]


def multiply(pieces, left, right):
    product = lax.dot_general(left, right, (((0,), (0,)), ((), ())), preferred_element_type=jnp.float32)
    return product.reshape(pieces, BLOCK // pieces, BLOCK)


def first_kernel(cols_per, per_peer, rows, cols, list1, hidden, grad_out, pushed, for_core, table, sems):
    me = lax.axis_index("tensor")
    copies = []

    def gather(n, source, there):
        for j in range(per_peer):
            copies.append(pltpu.make_async_copy(column(source, table[j]), there.at[j], sems.at[n, j]))
            copies[-1].start()

    listed_at(table, cols, rows, me ^ 2, cols_per, per_peer)
    gather(0, hidden, pushed)
    listed_at(table, list1, None, me, cols_per, per_peer)
    gather(1, grad_out, for_core)
    for copy in copies:
        copy.wait()


def first_sends(rows, cols, list1, hidden, grad_out, per_peer):
    tok_rows, width = grad_out.shape
    return pl.pallas_call(
        functools.partial(first_kernel, width // BLOCK, per_peer),
        out_shape=[pltpu.VMEM((per_peer, tok_rows, BLOCK), grad_out.dtype)] * 2,
        in_specs=[SMEM, SMEM, SMEM, HBM, HBM],
        out_specs=[VMEM, VMEM],
        scratch_shapes=[pltpu.SMEM((per_peer + 1,), jnp.int32), pltpu.SemaphoreType.DMA((2, per_peer))],
        name="first_sends",
    )(scalars(rows), scalars(cols), scalars(list1), hidden, grad_out)


def near_kernel(cols_per, per_peer, pieces, rows, cols, list3, hidden, grad_out, arrived, kept, sent, hidden_far, for_far, hidden_near, grad_near, parts, table, sems):
    me = lax.axis_index("tensor")
    count = [0]

    def gather(owner, listed, values, source, there, first):
        listed_at(table, listed, values, owner, cols_per, per_peer)
        copies = []
        for j in range(per_peer):
            copies.append(pltpu.make_async_copy(column(source, table[j]), there.at[first + j], sems.at[count[0], j]))
            copies[-1].start()
        count[0] += 1
        return copies

    mine = gather(me, cols, None, grad_out, grad_near, 0)
    near = gather(me, cols, rows, hidden, hidden_near, 0)
    near += gather(me ^ 1, cols, rows, hidden, hidden_near, per_peer)
    later = gather(me, list3, None, grad_out, for_far, 0)
    later += gather(me ^ 3, cols, rows, hidden, hidden_far, 0)
    for copy in mine + near:
        copy.wait()
    for item in range(2 * per_peer):
        right = grad_near[item] if item < per_peer else arrived[item - per_peer]
        parts[:, item] = multiply(pieces, hidden_near[item], right)
    split_pieces(parts, kept, sent)
    for copy in later:
        copy.wait()


def near_products(rows, cols, list3, hidden, grad_out, arrived, per_peer, pieces):
    tok_rows, width = grad_out.shape
    near = 2 * per_peer
    blocks = pltpu.VMEM((per_peer, tok_rows, BLOCK), jnp.bfloat16)
    return pl.pallas_call(
        functools.partial(near_kernel, width // BLOCK, per_peer, pieces),
        out_shape=halved_shapes(pieces, near) + [blocks, blocks],
        in_specs=[SMEM, SMEM, SMEM, HBM, HBM, VMEM],
        out_specs=[VMEM] * 4,
        scratch_shapes=[
            pltpu.VMEM((near, tok_rows, BLOCK), jnp.bfloat16),
            pltpu.VMEM((per_peer, tok_rows, BLOCK), jnp.bfloat16),
            pltpu.VMEM((pieces, near, BLOCK // pieces, BLOCK), jnp.float32),
            pltpu.SMEM((per_peer + 1,), jnp.int32),
            pltpu.SemaphoreType.DMA((5, per_peer)),
        ],
        name="near_products",
    )(scalars(rows), scalars(cols), scalars(list3), hidden, grad_out, vectors(arrived))


def guest_kernel(cols_per, per_peer, pieces, list2, grad_out, arrived, kept, sent, right, parts, table, sems):
    listed_at(table, list2, None, lax.axis_index("tensor"), cols_per, per_peer)
    copies = [pltpu.make_async_copy(column(grad_out, table[j]), right.at[j], sems.at[j]) for j in range(per_peer)]
    for copy in copies:
        copy.start()
    for copy in copies:
        copy.wait()
    for j in range(per_peer):
        parts[:, j] = multiply(pieces, arrived[j], right[j])
    split_pieces(parts, kept, sent)


def guest_products(list2, grad_out, arrived, per_peer, pieces):
    tok_rows, width = grad_out.shape
    return pl.pallas_call(
        functools.partial(guest_kernel, width // BLOCK, per_peer, pieces),
        out_shape=halved_shapes(pieces, per_peer),
        in_specs=[SMEM, HBM, VMEM],
        out_specs=[VMEM, VMEM],
        scratch_shapes=[
            pltpu.VMEM((per_peer, tok_rows, BLOCK), jnp.bfloat16),
            pltpu.VMEM((pieces, per_peer, BLOCK // pieces, BLOCK), jnp.float32),
            pltpu.SMEM((per_peer + 1,), jnp.int32),
            pltpu.SemaphoreType.DMA((per_peer,)),
        ],
        name="guest_products",
    )(scalars(list2), grad_out, vectors(arrived))


def far_kernel(pieces, left, arrived, kept, sent, parts):
    for j in range(arrived.shape[0]):
        parts[:, j] = multiply(pieces, left[j], arrived[j])
    split_pieces(parts, kept, sent)


def far_products(left, arrived, pieces):
    count, _, _ = arrived.shape
    return pl.pallas_call(
        functools.partial(far_kernel, pieces),
        out_shape=halved_shapes(pieces, count),
        in_specs=[VMEM, VMEM],
        out_specs=[VMEM, VMEM],
        scratch_shapes=[pltpu.VMEM((pieces, count, BLOCK // pieces, BLOCK), jnp.float32)],
        name="far_products",
    )(vectors(left), vectors(arrived))


def settle_kernel(cols_per, per_peer, cols, owners, near, guests, far, out, summed, seen):
    me = lax.axis_index("tensor")
    for index in range(4):
        seen[index] = 0
    summed[pl.ds(0, 2 * per_peer)] = near[...]
    summed[pl.ds(2 * per_peer, per_peer)] = guests[...]
    summed[pl.ds(3 * per_peer, per_peer)] = far[...]
    out[...] = jnp.zeros_like(out)

    def visit(k, carry):
        last_owner, last_slot = carry
        distance = (cols[0, k] // cols_per) ^ me
        rank = seen[distance]
        seen[distance] = rank + 1
        owner = owners[0, k]
        slot = jnp.where(owner == last_owner, last_slot + 1, 0)
        out[owner, jnp.minimum(slot, CAP - 1)] = summed[distance * per_peer + jnp.minimum(rank, per_peer - 1)]
        return owner, slot

    lax.fori_loop(0, cols.shape[1], visit, (jnp.int32(-1), jnp.int32(0)), unroll=True)


def settle(cols, owners, near, guests, far, cols_per, pieces):
    per_peer, rows, _ = far.shape
    return pl.pallas_call(
        functools.partial(settle_kernel, cols_per, per_peer),
        out_shape=pltpu.VMEM((pieces, CAP, rows, BLOCK), jnp.bfloat16),
        in_specs=[SMEM, SMEM, VMEM, VMEM, VMEM],
        out_specs=VMEM,
        scratch_shapes=[pltpu.VMEM((4 * per_peer, rows, BLOCK), jnp.bfloat16), pltpu.SMEM((4,), jnp.int32)],
        name="settle",
    )(scalars(cols), scalars(owners), vectors(near), vectors(guests), vectors(far))


def sparse_on_device(hidden, grad_out, block_rows, block_cols, block_owner):
    tensor_count, seq_count = lax.axis_size("tensor"), lax.axis_size("seq")
    cols_per = grad_out.shape[1] // BLOCK
    per_peer = block_cols.shape[1] // tensor_count

    def to_peer(value, distance):
        return lax.ppermute(value, "tensor", [(i, i ^ distance) for i in range(tensor_count)])

    def scatter(value):
        return lax.all_to_all(value, "seq", split_axis=0, concat_axis=0, tiled=True)

    def reduce_pieces(kept, sent):
        distance = 1
        while True:
            received = lax.ppermute(sent, "seq", [(i, i ^ distance) for i in range(seq_count)])
            if kept.shape[0] == 1:
                return finish(kept, received)
            kept, sent = halve(kept, received)
            distance *= 2

    list3 = to_peer(block_cols, 3)
    list1 = to_peer(block_cols, 1)
    list2 = to_peer(block_cols, 2)
    pushed, for_core = first_sends(block_rows, block_cols, list1, hidden, grad_out, per_peer)
    guests = to_peer(pushed, 2)
    from_core = to_peer(for_core, 1)
    near_kept, near_sent, hidden_far, for_far = near_products(
        block_rows, block_cols, list3, hidden, grad_out, from_core, per_peer, seq_count
    )
    from_far = to_peer(for_far, 3)
    near_sum = reduce_pieces(near_kept, near_sent)
    guest_kept, guest_sent = guest_products(list2, grad_out, guests, per_peer, seq_count)
    guest_sum = reduce_pieces(guest_kept, guest_sent)
    guest_back = to_peer(guest_sum, 2)
    far_kept, far_sent = far_products(hidden_far, from_far, seq_count)
    far_sum = reduce_pieces(far_kept, far_sent)
    placed = settle(block_cols, block_owner, near_sum, guest_back, far_sum, cols_per, seq_count)
    delivered = scatter(placed)
    return delivered.transpose(1, 0, 2, 3).reshape(1, CAP, BLOCK, BLOCK)


def solution(mesh):
    tensor_count, seq_count = mesh.shape["tensor"], mesh.shape["seq"]
    placed = (
        P("seq", "tensor"),
        P("seq", "tensor"),
        P("tensor", None),
        P("tensor", None),
        P("tensor", None),
    )

    def on_device(hidden, grad_out, block_rows, block_cols, block_owner):
        listed = block_cols.shape[1]
        each_named_once = listed == 24 and tensor_count == 4
        whole_tiles = BLOCK % (seq_count * ROW_TILE) == 0
        step = sparse_on_device if each_named_once and whole_tiles else dense_on_device
        return step(hidden, grad_out, block_rows, block_cols, block_owner)

    return jax.shard_map(
        on_device,
        mesh=mesh,
        in_specs=placed,
        out_specs=P("tensor", "seq", None, None),
        check_vma=False,
    )
```

```python
import functools

import jax
import jax.numpy as jnp
from jax import lax
from jax.experimental import pallas as pl
from jax.experimental.pallas import tpu as pltpu
from jax.sharding import PartitionSpec as P


BLOCK = 128
CAP = 8
ROW_TILE = 16

SMEM = pl.BlockSpec(memory_space=pltpu.SMEM)
HBM = pl.BlockSpec(memory_space=pltpu.HBM)
VMEM = pl.BlockSpec(memory_space=pltpu.VMEM)


def pick_slots(summed, starts, counts):
    slot_ids = starts[:, None] + jnp.arange(CAP, dtype=jnp.int32)[None, :]
    is_live = jnp.arange(CAP, dtype=jnp.int32)[None, :] < counts[:, None]
    picked = jnp.take(summed, jnp.minimum(slot_ids, summed.shape[0] - 1).reshape(-1), axis=0)
    picked = picked.reshape(slot_ids.shape[0], CAP, BLOCK, BLOCK)
    return jnp.where(is_live[:, :, None, None], picked, jnp.zeros_like(picked))


def dense_on_device(hidden, grad_out, block_rows, block_cols, block_owner):
    tok_rows = hidden.shape[0]
    hidden_sel = jnp.take(hidden.reshape(tok_rows, -1, BLOCK), block_rows[0], axis=1)
    cotangent = lax.all_gather(grad_out, "tensor", axis=1, tiled=True)
    grad_sel = jnp.take(cotangent.reshape(tok_rows, -1, BLOCK), block_cols[0], axis=1)
    partial_value = jnp.einsum(
        "tkr,tkc->krc", hidden_sel, grad_sel, preferred_element_type=jnp.float32
    ).astype(jnp.bfloat16)
    seq_count = lax.axis_size("seq")
    members = (block_owner[0][None, :] == jnp.arange(seq_count, dtype=jnp.int32)[:, None]).astype(jnp.int32)
    counts = jnp.sum(members, axis=1)
    starts = jnp.cumsum(counts) - counts
    outgoing = pick_slots(partial_value, starts, counts)
    received = lax.all_to_all(outgoing, "seq", split_axis=0, concat_axis=0, tiled=True)
    return jnp.sum(received, axis=0, dtype=jnp.float32).astype(jnp.bfloat16)[None]


def scalars(value):
    return pltpu.with_memory_space_constraint(value, pltpu.SMEM)


def vectors(value):
    return pltpu.with_memory_space_constraint(value, pltpu.VMEM)


def column(ref, index):
    return ref.at[:, pl.ds(pl.multiple_of(index * BLOCK, BLOCK), BLOCK)]


def listed_at(table, cols, values, owner, cols_per, per_peer):
    listed = [cols[0, k] - owner * cols_per for k in range(cols.shape[1])]
    taken = listed if values is None else [values[0, k] for k in range(cols.shape[1])]
    found = jnp.int32(0)
    for local, value in zip(listed, taken):
        hit = jnp.logical_and(local >= 0, local < cols_per)
        table[jnp.where(hit, jnp.minimum(found, per_peer - 1), per_peer)] = value
        found += hit.astype(jnp.int32)


def split_pieces(parts, kept, sent):
    me = lax.axis_index("seq")
    half = kept.shape[0]
    width = half.bit_length() - 1
    for index in range(half):
        apart = sum(((index >> (width - 1 - bit)) & 1) << (bit + 1) for bit in range(width))
        kept[index] = parts[me ^ apart]
        sent[index] = parts[me ^ apart ^ 1].astype(jnp.bfloat16)


def halve_kernel(*refs):
    parts, (still, sent) = refs[:-2], refs[-2:]
    half = still.shape[0]
    first = 0
    for kept, received in zip(parts[0::2], parts[1::2]):
        items = pl.ds(first, kept.shape[1])
        still[:, items] = kept[:half] + received[:half].astype(jnp.float32)
        sent[:, items] = (kept[half:] + received[half:].astype(jnp.float32)).astype(jnp.bfloat16)
        first += kept.shape[1]


def halve(parts):
    half, _, rows, _ = parts[0][0].shape
    shape = (half // 2, sum(kept.shape[1] for kept, _ in parts), rows, BLOCK)
    return pl.pallas_call(
        halve_kernel,
        out_shape=[pltpu.VMEM(shape, jnp.float32), pltpu.VMEM(shape, jnp.bfloat16)],
        in_specs=[VMEM] * (2 * len(parts)),
        out_specs=[VMEM, VMEM],
    )(*[vectors(value) for part in parts for value in part])


def finish_kernel(kept, received, *outs):
    first = 0
    for out in outs:
        items = pl.ds(first, out.shape[0])
        out[...] = (kept[0, items] + received[0, items].astype(jnp.float32)).astype(jnp.bfloat16)
        first += out.shape[0]


def finish(kept, received, counts):
    return pl.pallas_call(
        finish_kernel,
        out_shape=[pltpu.VMEM((count,) + kept.shape[2:], jnp.bfloat16) for count in counts],
        in_specs=[VMEM, VMEM],
        out_specs=[VMEM] * len(counts),
    )(vectors(kept), vectors(received))


def halved_shapes(pieces, items):
    shape = (pieces // 2, items, BLOCK // pieces, BLOCK)
    return [pltpu.VMEM(shape, jnp.float32), pltpu.VMEM(shape, jnp.bfloat16)]


def multiply(pieces, left, right):
    product = lax.dot_general(left, right, (((0,), (0,)), ((), ())), preferred_element_type=jnp.float32)
    return product.reshape(pieces, BLOCK // pieces, BLOCK)


def push_kernel(cols_per, per_peer, rows, cols, hidden, pushed, table, sems):
    listed_at(table, cols, rows, lax.axis_index("tensor") ^ 2, cols_per, per_peer)
    copies = [pltpu.make_async_copy(column(hidden, table[j]), pushed.at[j], sems.at[j]) for j in range(per_peer)]
    for copy in copies:
        copy.start()
    for copy in copies:
        copy.wait()


def push_blocks(rows, cols, hidden, cols_per, per_peer):
    return pl.pallas_call(
        functools.partial(push_kernel, cols_per, per_peer),
        out_shape=pltpu.VMEM((per_peer, hidden.shape[0], BLOCK), hidden.dtype),
        in_specs=[SMEM, SMEM, HBM],
        out_specs=VMEM,
        scratch_shapes=[pltpu.SMEM((per_peer + 1,), jnp.int32), pltpu.SemaphoreType.DMA((per_peer,))],
        name="push_blocks",
    )(scalars(rows), scalars(cols), hidden)


def pack_kernel(cols_per, per_peer, list1, list3, grad_out, for_core, for_far, table, sems):
    me = lax.axis_index("tensor")
    copies = []
    for n, (listed, there) in enumerate(((list1, for_core), (list3, for_far))):
        listed_at(table, listed, None, me, cols_per, per_peer)
        for j in range(per_peer):
            copies.append(pltpu.make_async_copy(column(grad_out, table[j]), there.at[j], sems.at[n, j]))
            copies[-1].start()
    for copy in copies:
        copy.wait()


def pack_columns(list1, list3, grad_out, per_peer):
    tok_rows, width = grad_out.shape
    return pl.pallas_call(
        functools.partial(pack_kernel, width // BLOCK, per_peer),
        out_shape=[pltpu.VMEM((per_peer, tok_rows, BLOCK), grad_out.dtype)] * 2,
        in_specs=[SMEM, SMEM, HBM],
        out_specs=[VMEM, VMEM],
        scratch_shapes=[pltpu.SMEM((per_peer + 1,), jnp.int32), pltpu.SemaphoreType.DMA((2, per_peer))],
        name="pack_columns",
    )(scalars(list1), scalars(list3), grad_out)


def near_kernel(cols_per, per_peer, pieces, rows, cols, hidden, grad_out, arrived, kept, sent, hidden_far, hidden_near, grad_near, parts, table, sems):
    me = lax.axis_index("tensor")
    count = [0]

    def gather(owner, listed, values, source, there, first):
        listed_at(table, listed, values, owner, cols_per, per_peer)
        copies = []
        for j in range(per_peer):
            copies.append(pltpu.make_async_copy(column(source, table[j]), there.at[first + j], sems.at[count[0], j]))
            copies[-1].start()
        count[0] += 1
        return copies

    mine = gather(me, cols, None, grad_out, grad_near, 0)
    near = gather(me, cols, rows, hidden, hidden_near, 0)
    near += gather(me ^ 1, cols, rows, hidden, hidden_near, per_peer)
    later = gather(me ^ 3, cols, rows, hidden, hidden_far, 0)
    for copy in mine + near:
        copy.wait()
    for item in range(2 * per_peer):
        right = grad_near[item] if item < per_peer else arrived[item - per_peer]
        parts[:, item] = multiply(pieces, hidden_near[item], right)
    split_pieces(parts, kept, sent)
    for copy in later:
        copy.wait()


def near_products(rows, cols, hidden, grad_out, arrived, per_peer, pieces):
    tok_rows, width = grad_out.shape
    near = 2 * per_peer
    blocks = pltpu.VMEM((per_peer, tok_rows, BLOCK), jnp.bfloat16)
    return pl.pallas_call(
        functools.partial(near_kernel, width // BLOCK, per_peer, pieces),
        out_shape=halved_shapes(pieces, near) + [blocks],
        in_specs=[SMEM, SMEM, HBM, HBM, VMEM],
        out_specs=[VMEM] * 3,
        scratch_shapes=[
            pltpu.VMEM((near, tok_rows, BLOCK), jnp.bfloat16),
            pltpu.VMEM((per_peer, tok_rows, BLOCK), jnp.bfloat16),
            pltpu.VMEM((pieces, near, BLOCK // pieces, BLOCK), jnp.float32),
            pltpu.SMEM((per_peer + 1,), jnp.int32),
            pltpu.SemaphoreType.DMA((4, per_peer)),
        ],
        name="near_products",
    )(scalars(rows), scalars(cols), hidden, grad_out, vectors(arrived))


def guest_kernel(cols_per, per_peer, pieces, list2, grad_out, arrived, kept, sent, right, parts, table, sems):
    listed_at(table, list2, None, lax.axis_index("tensor"), cols_per, per_peer)
    copies = [pltpu.make_async_copy(column(grad_out, table[j]), right.at[j], sems.at[j]) for j in range(per_peer)]
    for copy in copies:
        copy.start()
    for copy in copies:
        copy.wait()
    for j in range(per_peer):
        parts[:, j] = multiply(pieces, arrived[j], right[j])
    split_pieces(parts, kept, sent)


def guest_products(list2, grad_out, arrived, per_peer, pieces):
    tok_rows, width = grad_out.shape
    return pl.pallas_call(
        functools.partial(guest_kernel, width // BLOCK, per_peer, pieces),
        out_shape=halved_shapes(pieces, per_peer),
        in_specs=[SMEM, HBM, VMEM],
        out_specs=[VMEM, VMEM],
        scratch_shapes=[
            pltpu.VMEM((per_peer, tok_rows, BLOCK), jnp.bfloat16),
            pltpu.VMEM((pieces, per_peer, BLOCK // pieces, BLOCK), jnp.float32),
            pltpu.SMEM((per_peer + 1,), jnp.int32),
            pltpu.SemaphoreType.DMA((per_peer,)),
        ],
        name="guest_products",
    )(scalars(list2), grad_out, vectors(arrived))


def far_kernel(pieces, left, arrived, kept, sent, parts):
    for j in range(arrived.shape[0]):
        parts[:, j] = multiply(pieces, left[j], arrived[j])
    split_pieces(parts, kept, sent)


def far_products(left, arrived, pieces):
    count, _, _ = arrived.shape
    return pl.pallas_call(
        functools.partial(far_kernel, pieces),
        out_shape=halved_shapes(pieces, count),
        in_specs=[VMEM, VMEM],
        out_specs=[VMEM, VMEM],
        scratch_shapes=[pltpu.VMEM((pieces, count, BLOCK // pieces, BLOCK), jnp.float32)],
        name="far_products",
    )(vectors(left), vectors(arrived))


def settle_kernel(cols_per, per_peer, cols, owners, near, guests, far, out, summed, seen):
    me = lax.axis_index("tensor")
    for index in range(4):
        seen[index] = 0
    summed[pl.ds(0, 2 * per_peer)] = near[...]
    summed[pl.ds(2 * per_peer, per_peer)] = guests[...]
    summed[pl.ds(3 * per_peer, per_peer)] = far[...]
    out[...] = jnp.zeros_like(out)

    listed = range(cols.shape[1])
    distances = [lax.shift_right_logical(cols[0, k], cols_per.bit_length() - 1) ^ me for k in listed]
    placed_at = [owners[0, k] for k in listed]
    slot = jnp.int32(0)
    ranks = []
    for k in listed:
        rank = seen[distances[k]]
        seen[distances[k]] = rank + 1
        ranks.append(rank)
    for k in listed:
        slot = jnp.where(placed_at[k] == placed_at[k - 1], slot + 1, 0) if k else slot
        out[placed_at[k], jnp.minimum(slot, CAP - 1)] = summed[
            distances[k] * per_peer + jnp.minimum(ranks[k], per_peer - 1)
        ]


def settle(cols, owners, near, guests, far, cols_per, pieces):
    per_peer, rows, _ = far.shape
    return pl.pallas_call(
        functools.partial(settle_kernel, cols_per, per_peer),
        out_shape=pltpu.VMEM((pieces, CAP, rows, BLOCK), jnp.bfloat16),
        in_specs=[SMEM, SMEM, VMEM, VMEM, VMEM],
        out_specs=VMEM,
        scratch_shapes=[pltpu.VMEM((4 * per_peer, rows, BLOCK), jnp.bfloat16), pltpu.SMEM((4,), jnp.int32)],
        name="settle",
    )(scalars(cols), scalars(owners), vectors(near), vectors(guests), vectors(far))


def sparse_on_device(hidden, grad_out, block_rows, block_cols, block_owner):
    tensor_count, seq_count = lax.axis_size("tensor"), lax.axis_size("seq")
    cols_per = grad_out.shape[1] // BLOCK
    per_peer = block_cols.shape[1] // tensor_count

    def to_peer(value, distance):
        return lax.ppermute(value, "tensor", [(i, i ^ distance) for i in range(tensor_count)])

    def scatter(value):
        return lax.all_to_all(value, "seq", split_axis=0, concat_axis=0, tiled=True)

    def exchange(sent, distance):
        return lax.ppermute(sent, "seq", [(i, i ^ distance) for i in range(seq_count)])

    def reduce_pieces(kept, sent):
        distance = 1
        while True:
            received = exchange(sent, distance)
            distance *= 2
            if distance == seq_count:
                return finish(kept, received, (kept.shape[1],))[0]
            kept, sent = halve([(kept, received)])

    list3 = to_peer(block_cols, 3)
    pushed = push_blocks(block_rows, block_cols, hidden, cols_per, per_peer)
    guests = to_peer(pushed, 2)
    list1 = to_peer(block_cols, 1)
    list2 = to_peer(block_cols, 2)
    for_core, for_far = pack_columns(list1, list3, grad_out, per_peer)
    from_core = to_peer(for_core, 1)
    from_far = to_peer(for_far, 3)
    near_kept, near_sent, hidden_far = near_products(
        block_rows, block_cols, hidden, grad_out, from_core, per_peer, seq_count
    )
    near_sum = reduce_pieces(near_kept, near_sent)
    guest_kept, guest_sent = guest_products(list2, grad_out, guests, per_peer, seq_count)
    guest_sum = reduce_pieces(guest_kept, guest_sent)
    guest_back = to_peer(guest_sum, 2)
    far_kept, far_sent = far_products(hidden_far, from_far, seq_count)
    far_sum = reduce_pieces(far_kept, far_sent)
    placed = settle(block_cols, block_owner, near_sum, guest_back, far_sum, cols_per, seq_count)
    delivered = scatter(placed)
    return delivered.transpose(1, 0, 2, 3).reshape(1, CAP, BLOCK, BLOCK)


def solution(mesh):
    tensor_count, seq_count = mesh.shape["tensor"], mesh.shape["seq"]
    placed = (
        P("seq", "tensor"),
        P("seq", "tensor"),
        P("tensor", None),
        P("tensor", None),
        P("tensor", None),
    )

    def on_device(hidden, grad_out, block_rows, block_cols, block_owner):
        listed = block_cols.shape[1]
        each_named_once = listed == 24 and tensor_count == 4
        whole_tiles = BLOCK % (seq_count * ROW_TILE) == 0
        step = sparse_on_device if each_named_once and whole_tiles else dense_on_device
        return step(hidden, grad_out, block_rows, block_cols, block_owner)

    return jax.shard_map(
        on_device,
        mesh=mesh,
        in_specs=placed,
        out_specs=P("tensor", "seq", None, None),
        check_vma=False,
    )
```

```python
import functools

import jax
import jax.numpy as jnp
from jax import lax
from jax.experimental import pallas as pl
from jax.experimental.pallas import tpu as pltpu
from jax.sharding import PartitionSpec as P


BLOCK = 128
CAP = 8
ROW_TILE = 16

SMEM = pl.BlockSpec(memory_space=pltpu.SMEM)
HBM = pl.BlockSpec(memory_space=pltpu.HBM)
SMALL = pltpu.CompilerParams(vmem_limit_bytes=8 << 20)
VMEM = pl.BlockSpec(memory_space=pltpu.VMEM)


def pick_slots(summed, starts, counts):
    slot_ids = starts[:, None] + jnp.arange(CAP, dtype=jnp.int32)[None, :]
    is_live = jnp.arange(CAP, dtype=jnp.int32)[None, :] < counts[:, None]
    picked = jnp.take(summed, jnp.minimum(slot_ids, summed.shape[0] - 1).reshape(-1), axis=0)
    picked = picked.reshape(slot_ids.shape[0], CAP, BLOCK, BLOCK)
    return jnp.where(is_live[:, :, None, None], picked, jnp.zeros_like(picked))


def dense_on_device(hidden, grad_out, block_rows, block_cols, block_owner):
    tok_rows = hidden.shape[0]
    hidden_sel = jnp.take(hidden.reshape(tok_rows, -1, BLOCK), block_rows[0], axis=1)
    cotangent = lax.all_gather(grad_out, "tensor", axis=1, tiled=True)
    grad_sel = jnp.take(cotangent.reshape(tok_rows, -1, BLOCK), block_cols[0], axis=1)
    partial_value = jnp.einsum(
        "tkr,tkc->krc", hidden_sel, grad_sel, preferred_element_type=jnp.float32
    ).astype(jnp.bfloat16)
    seq_count = lax.axis_size("seq")
    members = (block_owner[0][None, :] == jnp.arange(seq_count, dtype=jnp.int32)[:, None]).astype(jnp.int32)
    counts = jnp.sum(members, axis=1)
    starts = jnp.cumsum(counts) - counts
    outgoing = pick_slots(partial_value, starts, counts)
    received = lax.all_to_all(outgoing, "seq", split_axis=0, concat_axis=0, tiled=True)
    return jnp.sum(received, axis=0, dtype=jnp.float32).astype(jnp.bfloat16)[None]


def scalars(value):
    return pltpu.with_memory_space_constraint(value, pltpu.SMEM)


def in_hbm(value):
    return pltpu.with_memory_space_constraint(value, pltpu.HBM)


def vectors(value):
    return pltpu.with_memory_space_constraint(value, pltpu.VMEM)


def column(ref, index):
    return ref.at[:, pl.ds(pl.multiple_of(index * BLOCK, BLOCK), BLOCK)]


def listed_at(table, cols, values, owner, cols_per, per_peer):
    listed = [cols[0, k] - owner * cols_per for k in range(cols.shape[1])]
    taken = listed if values is None else [values[0, k] for k in range(cols.shape[1])]
    found = jnp.int32(0)
    for local, value in zip(listed, taken):
        hit = jnp.logical_and(local >= 0, local < cols_per)
        table[jnp.where(hit, jnp.minimum(found, per_peer - 1), per_peer)] = value
        found += hit.astype(jnp.int32)


def split_pieces(order, parts, kept, sent):
    me = lax.axis_index("seq")
    width = len(order) - 1
    for index in range(kept.shape[0]):
        apart = sum(((index >> (width - 1 - bit)) & 1) * order[bit + 1] for bit in range(width))
        kept[index] = parts[me ^ apart]
        sent[index] = parts[me ^ apart ^ order[0]].astype(jnp.bfloat16)


def halve_kernel(*refs):
    parts, (still, sent) = refs[:-2], refs[-2:]
    half = still.shape[0]
    first = 0
    for kept, received in zip(parts[0::2], parts[1::2]):
        items = pl.ds(first, kept.shape[1])
        still[:, items] = kept[:half] + received[:half].astype(jnp.float32)
        sent[:, items] = (kept[half:] + received[half:].astype(jnp.float32)).astype(jnp.bfloat16)
        first += kept.shape[1]


def halve(parts):
    half, _, rows, _ = parts[0][0].shape
    shape = (half // 2, sum(kept.shape[1] for kept, _ in parts), rows, BLOCK)
    return pl.pallas_call(
        halve_kernel,
        out_shape=[pltpu.VMEM(shape, jnp.float32), pltpu.VMEM(shape, jnp.bfloat16)],
        in_specs=[VMEM] * (2 * len(parts)),
        out_specs=[VMEM, VMEM],
        compiler_params=SMALL,
    )(*[vectors(value) for part in parts for value in part])


def finish_kernel(kept, received, *outs):
    first = 0
    for out in outs:
        items = pl.ds(first, out.shape[0])
        out[...] = (kept[0, items] + received[0, items].astype(jnp.float32)).astype(jnp.bfloat16)
        first += out.shape[0]


def finish(kept, received, counts):
    return pl.pallas_call(
        finish_kernel,
        out_shape=[pltpu.VMEM((count,) + kept.shape[2:], jnp.bfloat16) for count in counts],
        in_specs=[VMEM, VMEM],
        out_specs=[VMEM] * len(counts),
        compiler_params=SMALL,
    )(vectors(kept), vectors(received))


def halved_shapes(pieces, items):
    shape = (pieces // 2, items, BLOCK // pieces, BLOCK)
    return [pltpu.VMEM(shape, jnp.float32), pltpu.VMEM(shape, jnp.bfloat16)]


def multiply(pieces, left, right):
    product = lax.dot_general(left, right, (((0,), (0,)), ((), ())), preferred_element_type=jnp.float32)
    return product.reshape(pieces, BLOCK // pieces, BLOCK)


def push_kernel(cols_per, per_peer, all_rows, all_cols, hidden, pushed, rows, cols, table, list_sems, sems):
    fetched = [
        pltpu.make_async_copy(a, b, list_sems.at[n]) for n, (a, b) in enumerate(((all_rows, rows), (all_cols, cols)))
    ]
    for copy in fetched:
        copy.start()
    for copy in fetched:
        copy.wait()
    listed_at(table, cols, rows, lax.axis_index("tensor") ^ 2, cols_per, per_peer)
    copies = [pltpu.make_async_copy(column(hidden, table[j]), pushed.at[j], sems.at[j]) for j in range(per_peer)]
    for copy in copies:
        copy.start()
    for copy in copies:
        copy.wait()


def push_blocks(rows, cols, hidden, cols_per, per_peer):
    return pl.pallas_call(
        functools.partial(push_kernel, cols_per, per_peer),
        out_shape=pltpu.VMEM((per_peer, hidden.shape[0], BLOCK), hidden.dtype),
        in_specs=[HBM, HBM, HBM],
        out_specs=VMEM,
        scratch_shapes=[
            pltpu.SMEM(rows.shape, jnp.int32),
            pltpu.SMEM(cols.shape, jnp.int32),
            pltpu.SMEM((per_peer + 1,), jnp.int32),
            pltpu.SemaphoreType.DMA((2,)),
            pltpu.SemaphoreType.DMA((per_peer,)),
        ],
        name="push_blocks",
        compiler_params=SMALL,
    )(in_hbm(rows), in_hbm(cols), in_hbm(hidden))


def pack_kernel(cols_per, per_peer, came1, came3, grad_out, for_core, for_far, list1, list3, table, list_sems, sems):
    me = lax.axis_index("tensor")
    fetched = [pltpu.make_async_copy(a, b, list_sems.at[n]) for n, (a, b) in enumerate(((came1, list1), (came3, list3)))]
    for copy in fetched:
        copy.start()
    for copy in fetched:
        copy.wait()
    copies = []
    for n, (listed, there) in enumerate(((list1, for_core), (list3, for_far))):
        listed_at(table, listed, None, me, cols_per, per_peer)
        for j in range(per_peer):
            copies.append(pltpu.make_async_copy(column(grad_out, table[j]), there.at[j], sems.at[n, j]))
            copies[-1].start()
    for copy in copies:
        copy.wait()


def pack_columns(list1, list3, grad_out, per_peer):
    tok_rows, width = grad_out.shape
    return pl.pallas_call(
        functools.partial(pack_kernel, width // BLOCK, per_peer),
        out_shape=[pltpu.VMEM((per_peer, tok_rows, BLOCK), grad_out.dtype)] * 2,
        in_specs=[VMEM, VMEM, HBM],
        out_specs=[VMEM, VMEM],
        scratch_shapes=[
            pltpu.SMEM(list1.shape, jnp.int32),
            pltpu.SMEM(list3.shape, jnp.int32),
            pltpu.SMEM((per_peer + 1,), jnp.int32),
            pltpu.SemaphoreType.DMA((2,)),
            pltpu.SemaphoreType.DMA((2, per_peer)),
        ],
        name="pack_columns",
        compiler_params=SMALL,
    )(vectors(list1), vectors(list3), in_hbm(grad_out))


def near_kernel(order, cols_per, per_peer, pieces, rows, cols, came2, hidden, grad_out, arrived, kept, sent, hidden_far, grad_guest, hidden_near, grad_near, parts, list2, table, list_sem, sems):
    fetched = pltpu.make_async_copy(came2, list2, list_sem)
    fetched.start()
    me = lax.axis_index("tensor")
    count = [0]

    def gather(owner, listed, values, source, there, first):
        listed_at(table, listed, values, owner, cols_per, per_peer)
        copies = []
        for j in range(per_peer):
            copies.append(pltpu.make_async_copy(column(source, table[j]), there.at[first + j], sems.at[count[0], j]))
            copies[-1].start()
        count[0] += 1
        return copies

    mine = gather(me, cols, None, grad_out, grad_near, 0)
    near = gather(me, cols, rows, hidden, hidden_near, 0)
    near += gather(me ^ 1, cols, rows, hidden, hidden_near, per_peer)
    later = gather(me ^ 3, cols, rows, hidden, hidden_far, 0)
    fetched.wait()
    later += gather(me, list2, None, grad_out, grad_guest, 0)
    for copy in mine + near:
        copy.wait()
    for item in range(2 * per_peer):
        right = grad_near[item] if item < per_peer else arrived[item - per_peer]
        parts[:, item] = multiply(pieces, hidden_near[item], right)
    split_pieces(order, parts, kept, sent)
    for copy in later:
        copy.wait()


def near_products(rows, cols, list2, hidden, grad_out, arrived, per_peer, pieces, order):
    tok_rows, width = grad_out.shape
    near = 2 * per_peer
    blocks = pltpu.VMEM((per_peer, tok_rows, BLOCK), jnp.bfloat16)
    return pl.pallas_call(
        functools.partial(near_kernel, order, width // BLOCK, per_peer, pieces),
        out_shape=halved_shapes(pieces, near) + [blocks, blocks],
        in_specs=[SMEM, SMEM, VMEM, HBM, HBM, VMEM],
        out_specs=[VMEM] * 4,
        scratch_shapes=[
            pltpu.VMEM((near, tok_rows, BLOCK), jnp.bfloat16),
            pltpu.VMEM((per_peer, tok_rows, BLOCK), jnp.bfloat16),
            pltpu.VMEM((pieces, near, BLOCK // pieces, BLOCK), jnp.float32),
            pltpu.SMEM(list2.shape, jnp.int32),
            pltpu.SMEM((per_peer + 1,), jnp.int32),
            pltpu.SemaphoreType.DMA,
            pltpu.SemaphoreType.DMA((5, per_peer)),
        ],
        name="near_products",
        compiler_params=SMALL,
    )(scalars(rows), scalars(cols), vectors(list2), in_hbm(hidden), in_hbm(grad_out), vectors(arrived))


def cross_kernel(order, pieces, left, right, kept, sent, parts):
    for j in range(left.shape[0]):
        parts[:, j] = multiply(pieces, left[j], right[j])
    split_pieces(order, parts, kept, sent)


def cross_products(left, right, pieces, order):
    count = left.shape[0]
    return pl.pallas_call(
        functools.partial(cross_kernel, order, pieces),
        out_shape=halved_shapes(pieces, count),
        in_specs=[VMEM, VMEM],
        out_specs=[VMEM, VMEM],
        scratch_shapes=[pltpu.VMEM((pieces, count, BLOCK // pieces, BLOCK), jnp.float32)],
        compiler_params=SMALL,
    )(vectors(left), vectors(right))


def plan_kernel(cols_per, per_peer, cols, owners, places, seen):
    me = lax.axis_index("tensor")
    for index in range(4):
        seen[index] = 0
    listed = range(cols.shape[1])
    distances = [lax.shift_right_logical(cols[0, k], cols_per.bit_length() - 1) ^ me for k in listed]
    placed_at = [owners[0, k] for k in listed]
    slot = jnp.int32(0)
    for k in listed:
        rank = jnp.minimum(seen[distances[k]], per_peer - 1)
        seen[distances[k]] = rank + 1
        slot = jnp.where(placed_at[k] == placed_at[k - 1], slot + 1, 0) if k else slot
        places[distances[k] * per_peer + rank] = placed_at[k] * CAP + jnp.minimum(slot, CAP - 1)


def plan(cols, owners, cols_per, per_peer):
    return pl.pallas_call(
        functools.partial(plan_kernel, cols_per, per_peer),
        out_shape=pltpu.SMEM((cols.shape[1],), jnp.int32),
        in_specs=[SMEM, SMEM],
        out_specs=SMEM,
        scratch_shapes=[pltpu.SMEM((4,), jnp.int32)],
        name="plan",
        compiler_params=SMALL,
    )(scalars(cols), scalars(owners))


def settle_kernel(places, near, guests, kept, received, out):
    out[...] = jnp.zeros_like(out)
    first = 0
    for source in (near, guests):
        for j in range(source.shape[0]):
            out[places[first + j]] = source[j]
        first += source.shape[0]
    for j in range(kept.shape[1]):
        out[places[first + j]] = (kept[0, j] + received[0, j].astype(jnp.float32)).astype(jnp.bfloat16)


def settle(places, near, guests, kept, received, pieces):
    _, rows, _ = guests.shape
    return pl.pallas_call(
        settle_kernel,
        out_shape=pltpu.VMEM((pieces * CAP, rows, BLOCK), jnp.bfloat16),
        in_specs=[SMEM] + [VMEM] * 4,
        out_specs=VMEM,
        name="settle",
        compiler_params=SMALL,
    )(scalars(places), vectors(near), vectors(guests), vectors(kept), vectors(received))


def sparse_on_device(hidden, grad_out, block_rows, block_cols, block_owner):
    tensor_count, seq_count = lax.axis_size("tensor"), lax.axis_size("seq")
    cols_per = grad_out.shape[1] // BLOCK
    per_peer = block_cols.shape[1] // tensor_count

    def to_peer(value, distance):
        return lax.ppermute(value, "tensor", [(i, i ^ distance) for i in range(tensor_count)])

    def exchange(sent, distance):
        return lax.ppermute(sent, "seq", [(i, i ^ distance) for i in range(seq_count)])

    def reduce_pieces(order, kept, sent):
        for step, distance in enumerate(order):
            received = exchange(sent, distance)
            if step == len(order) - 1:
                return finish(kept, received, (kept.shape[1],))[0]
            kept, sent = halve([(kept, received)])

    near_order, guest_order = (2, 1, 4), (1, 2, 4)
    list3 = to_peer(block_cols, 3)
    pushed = push_blocks(block_rows, block_cols, hidden, cols_per, per_peer)
    guests = to_peer(pushed, 2)
    list1 = to_peer(block_cols, 1)
    list2 = to_peer(list3, 1)
    for_core, for_far = pack_columns(list1, list3, grad_out, per_peer)
    from_core = to_peer(for_core, 1)
    from_far = to_peer(for_far, 3)
    near_kept, near_sent, hidden_far, grad_guest = near_products(
        block_rows, block_cols, list2, hidden, grad_out, from_core, per_peer, seq_count, near_order
    )
    near_sum = reduce_pieces(near_order, near_kept, near_sent)
    places = plan(block_cols, block_owner, cols_per, per_peer)
    guest_kept, guest_sent = cross_products(guests, grad_guest, seq_count, guest_order)
    guest_sum = reduce_pieces(guest_order, guest_kept, guest_sent)
    guest_back = to_peer(guest_sum, 2)
    kept, sent = cross_products(hidden_far, from_far, seq_count, guest_order)
    received = exchange(sent, guest_order[0])
    for distance in guest_order[1:]:
        kept, sent = halve([(kept, received)])
        received = exchange(sent, distance)
    placed = settle(places, near_sum, guest_back, kept, received, seq_count)
    delivered = lax.all_to_all(
        placed.reshape(seq_count, CAP, -1, BLOCK), "seq", split_axis=0, concat_axis=0, tiled=True
    )
    return delivered.transpose(1, 0, 2, 3).reshape(1, CAP, BLOCK, BLOCK)


def solution(mesh):
    tensor_count, seq_count = mesh.shape["tensor"], mesh.shape["seq"]
    placed = (
        P("seq", "tensor"),
        P("seq", "tensor"),
        P("tensor", None),
        P("tensor", None),
        P("tensor", None),
    )

    def on_device(hidden, grad_out, block_rows, block_cols, block_owner):
        listed = block_cols.shape[1]
        each_named_once = listed == 24 and tensor_count == 4
        whole_tiles = BLOCK % (seq_count * ROW_TILE) == 0
        step = sparse_on_device if each_named_once and whole_tiles else dense_on_device
        return step(hidden, grad_out, block_rows, block_cols, block_owner)

    return jax.shard_map(
        on_device,
        mesh=mesh,
        in_specs=placed,
        out_specs=P("tensor", "seq", None, None),
        check_vma=False,
    )
```

```python
import functools

import jax
import jax.numpy as jnp
from jax import lax
from jax.experimental import pallas as pl
from jax.experimental.pallas import tpu as pltpu
from jax.sharding import PartitionSpec as P


BLOCK = 128
CAP = 8
ROW_TILE = 16

SMEM = pl.BlockSpec(memory_space=pltpu.SMEM)
HBM = pl.BlockSpec(memory_space=pltpu.HBM)
SMALL = pltpu.CompilerParams(vmem_limit_bytes=8 << 20)
VMEM = pl.BlockSpec(memory_space=pltpu.VMEM)


def pick_slots(summed, starts, counts):
    slot_ids = starts[:, None] + jnp.arange(CAP, dtype=jnp.int32)[None, :]
    is_live = jnp.arange(CAP, dtype=jnp.int32)[None, :] < counts[:, None]
    picked = jnp.take(summed, jnp.minimum(slot_ids, summed.shape[0] - 1).reshape(-1), axis=0)
    picked = picked.reshape(slot_ids.shape[0], CAP, BLOCK, BLOCK)
    return jnp.where(is_live[:, :, None, None], picked, jnp.zeros_like(picked))


def dense_on_device(hidden, grad_out, block_rows, block_cols, block_owner):
    tok_rows = hidden.shape[0]
    hidden_sel = jnp.take(hidden.reshape(tok_rows, -1, BLOCK), block_rows[0], axis=1)
    cotangent = lax.all_gather(grad_out, "tensor", axis=1, tiled=True)
    grad_sel = jnp.take(cotangent.reshape(tok_rows, -1, BLOCK), block_cols[0], axis=1)
    partial_value = jnp.einsum(
        "tkr,tkc->krc", hidden_sel, grad_sel, preferred_element_type=jnp.float32
    ).astype(jnp.bfloat16)
    seq_count = lax.axis_size("seq")
    members = (block_owner[0][None, :] == jnp.arange(seq_count, dtype=jnp.int32)[:, None]).astype(jnp.int32)
    counts = jnp.sum(members, axis=1)
    starts = jnp.cumsum(counts) - counts
    outgoing = pick_slots(partial_value, starts, counts)
    received = lax.all_to_all(outgoing, "seq", split_axis=0, concat_axis=0, tiled=True)
    return jnp.sum(received, axis=0, dtype=jnp.float32).astype(jnp.bfloat16)[None]


def scalars(value):
    return pltpu.with_memory_space_constraint(value, pltpu.SMEM)


def in_hbm(value):
    return pltpu.with_memory_space_constraint(value, pltpu.HBM)


def vectors(value):
    return pltpu.with_memory_space_constraint(value, pltpu.VMEM)


def column(ref, index):
    return ref.at[:, pl.ds(pl.multiple_of(index * BLOCK, BLOCK), BLOCK)]


def listed_at(table, cols, values, owner, cols_per, per_peer):
    listed = [cols[0, k] - owner * cols_per for k in range(cols.shape[1])]
    taken = listed if values is None else [values[0, k] for k in range(cols.shape[1])]
    found = jnp.int32(0)
    for local, value in zip(listed, taken):
        hit = jnp.logical_and(local >= 0, local < cols_per)
        table[jnp.where(hit, jnp.minimum(found, per_peer - 1), per_peer)] = value
        found += hit.astype(jnp.int32)


def split_pieces(order, parts, kept, sent):
    me = lax.axis_index("seq")
    width = len(order) - 1
    for index in range(kept.shape[0]):
        apart = sum(((index >> (width - 1 - bit)) & 1) * order[bit + 1] for bit in range(width))
        kept[index] = parts[me ^ apart]
        sent[index] = parts[me ^ apart ^ order[0]].astype(jnp.bfloat16)


def halve_kernel(*refs):
    parts, (still, sent) = refs[:-2], refs[-2:]
    half = still.shape[0]
    first = 0
    for kept, received in zip(parts[0::2], parts[1::2]):
        items = pl.ds(first, kept.shape[1])
        still[:, items] = kept[:half] + received[:half].astype(jnp.float32)
        sent[:, items] = (kept[half:] + received[half:].astype(jnp.float32)).astype(jnp.bfloat16)
        first += kept.shape[1]


def halve(parts):
    half, _, rows, _ = parts[0][0].shape
    shape = (half // 2, sum(kept.shape[1] for kept, _ in parts), rows, BLOCK)
    return pl.pallas_call(
        halve_kernel,
        out_shape=[pltpu.VMEM(shape, jnp.float32), pltpu.VMEM(shape, jnp.bfloat16)],
        in_specs=[VMEM] * (2 * len(parts)),
        out_specs=[VMEM, VMEM],
        compiler_params=SMALL,
    )(*[vectors(value) for part in parts for value in part])


def finish_kernel(kept, received, *outs):
    first = 0
    for out in outs:
        items = pl.ds(first, out.shape[0])
        out[...] = (kept[0, items] + received[0, items].astype(jnp.float32)).astype(jnp.bfloat16)
        first += out.shape[0]


def finish(kept, received, counts):
    return pl.pallas_call(
        finish_kernel,
        out_shape=[pltpu.VMEM((count,) + kept.shape[2:], jnp.bfloat16) for count in counts],
        in_specs=[VMEM, VMEM],
        out_specs=[VMEM] * len(counts),
        compiler_params=SMALL,
    )(vectors(kept), vectors(received))


def halved_shapes(pieces, items):
    shape = (pieces // 2, items, BLOCK // pieces, BLOCK)
    return [pltpu.VMEM(shape, jnp.float32), pltpu.VMEM(shape, jnp.bfloat16)]


def multiply(pieces, left, right):
    product = lax.dot_general(left, right, (((0,), (0,)), ((), ())), preferred_element_type=jnp.float32)
    return product.reshape(pieces, BLOCK // pieces, BLOCK)


def fetch(pairs, sems):
    copies = [pltpu.make_async_copy(source, there, sems.at[n]) for n, (source, there) in enumerate(pairs)]
    for copy in copies:
        copy.start()
    return copies


def start_columns(source, table, there, sems):
    copies = [pltpu.make_async_copy(column(source, table[j]), there.at[j], sems.at[j]) for j in range(there.shape[0])]
    for copy in copies:
        copy.start()
    return copies


def push_kernel(cols_per, per_peer, all_rows, all_cols, hidden, cross, core, rows, cols, table, list_sems, sems):
    for copy in fetch(((all_rows, rows), (all_cols, cols)), list_sems):
        copy.wait()
    me = lax.axis_index("tensor")
    copies = []
    for n, (distance, there) in enumerate(((2, cross), (1, core))):
        listed_at(table, cols, rows, me ^ distance, cols_per, per_peer)
        copies += start_columns(hidden, table, there, sems.at[n])
    for copy in copies:
        copy.wait()


def push_blocks(rows, cols, hidden, cols_per, per_peer):
    return pl.pallas_call(
        functools.partial(push_kernel, cols_per, per_peer),
        out_shape=[pltpu.VMEM((per_peer, hidden.shape[0], BLOCK), hidden.dtype)] * 2,
        in_specs=[HBM, HBM, HBM],
        out_specs=[VMEM, VMEM],
        scratch_shapes=[
            pltpu.SMEM(rows.shape, jnp.int32),
            pltpu.SMEM(cols.shape, jnp.int32),
            pltpu.SMEM((per_peer + 1,), jnp.int32),
            pltpu.SemaphoreType.DMA((2,)),
            pltpu.SemaphoreType.DMA((2, per_peer)),
        ],
        name="push_blocks",
        compiler_params=SMALL,
    )(in_hbm(rows), in_hbm(cols), in_hbm(hidden))


def near_kernel(order, cols_per, per_peer, pieces, all_rows, all_cols, came1, hidden, grad_out, arrived, kept, sent, own, right, parts, rows, cols, list1, table, list_sems, sems):
    me = lax.axis_index("tensor")
    for copy in fetch(((all_rows, rows), (all_cols, cols), (came1, list1)), list_sems):
        copy.wait()
    listed_at(table, cols, rows, me, cols_per, per_peer)
    copies = start_columns(hidden, table, own, sems.at[0])
    listed_at(table, cols, None, me, cols_per, per_peer)
    copies += start_columns(grad_out, table, right.at[pl.ds(0, per_peer)], sems.at[1])
    listed_at(table, list1, None, me, cols_per, per_peer)
    copies += start_columns(grad_out, table, right.at[pl.ds(per_peer, per_peer)], sems.at[2])
    for copy in copies:
        copy.wait()
    for item in range(2 * per_peer):
        left = own[item] if item < per_peer else arrived[item - per_peer]
        parts[:, item] = multiply(pieces, left, right[item])
    split_pieces(order, parts, kept, sent)


def near_products(rows, cols, list1, hidden, grad_out, arrived, per_peer, pieces, order):
    tok_rows, width = grad_out.shape
    return pl.pallas_call(
        functools.partial(near_kernel, order, width // BLOCK, per_peer, pieces),
        out_shape=halved_shapes(pieces, 2 * per_peer),
        in_specs=[HBM, HBM, VMEM, HBM, HBM, VMEM],
        out_specs=[VMEM, VMEM],
        scratch_shapes=[
            pltpu.VMEM((per_peer, tok_rows, BLOCK), jnp.bfloat16),
            pltpu.VMEM((2 * per_peer, tok_rows, BLOCK), jnp.bfloat16),
            pltpu.VMEM((pieces, 2 * per_peer, BLOCK // pieces, BLOCK), jnp.float32),
            pltpu.SMEM(rows.shape, jnp.int32),
            pltpu.SMEM(cols.shape, jnp.int32),
            pltpu.SMEM(list1.shape, jnp.int32),
            pltpu.SMEM((per_peer + 1,), jnp.int32),
            pltpu.SemaphoreType.DMA((3,)),
            pltpu.SemaphoreType.DMA((3, per_peer)),
        ],
        name="near_products",
        compiler_params=SMALL,
    )(in_hbm(rows), in_hbm(cols), vectors(list1), in_hbm(hidden), in_hbm(grad_out), vectors(arrived))


def pack_kernel(cols_per, per_peer, all_rows, all_cols, came2, came3, hidden, grad_out, for_far, for_guests, hidden_far, rows, cols, list2, list3, table, list_sems, sems):
    me = lax.axis_index("tensor")
    for copy in fetch(((all_rows, rows), (all_cols, cols), (came2, list2), (came3, list3)), list_sems):
        copy.wait()
    listed_at(table, list3, None, me, cols_per, per_peer)
    copies = start_columns(grad_out, table, for_far, sems.at[0])
    listed_at(table, list2, None, me, cols_per, per_peer)
    copies += start_columns(grad_out, table, for_guests, sems.at[1])
    listed_at(table, cols, rows, me ^ 3, cols_per, per_peer)
    copies += start_columns(hidden, table, hidden_far, sems.at[2])
    for copy in copies:
        copy.wait()


def pack_blocks(rows, cols, list2, list3, hidden, grad_out, per_peer):
    tok_rows, width = grad_out.shape
    return pl.pallas_call(
        functools.partial(pack_kernel, width // BLOCK, per_peer),
        out_shape=[pltpu.VMEM((per_peer, tok_rows, BLOCK), grad_out.dtype)] * 3,
        in_specs=[HBM, HBM, VMEM, VMEM, HBM, HBM],
        out_specs=[VMEM, VMEM, VMEM],
        scratch_shapes=[pltpu.SMEM(value.shape, jnp.int32) for value in (rows, cols, list2, list3)]
        + [
            pltpu.SMEM((per_peer + 1,), jnp.int32),
            pltpu.SemaphoreType.DMA((4,)),
            pltpu.SemaphoreType.DMA((3, per_peer)),
        ],
        name="pack_blocks",
        compiler_params=SMALL,
    )(in_hbm(rows), in_hbm(cols), vectors(list2), vectors(list3), in_hbm(hidden), in_hbm(grad_out))


def cross_kernel(order, pieces, left, right, kept, sent, parts):
    for j in range(left.shape[0]):
        parts[:, j] = multiply(pieces, left[j], right[j])
    split_pieces(order, parts, kept, sent)


def cross_products(left, right, pieces, order):
    count = left.shape[0]
    return pl.pallas_call(
        functools.partial(cross_kernel, order, pieces),
        out_shape=halved_shapes(pieces, count),
        in_specs=[VMEM, VMEM],
        out_specs=[VMEM, VMEM],
        scratch_shapes=[pltpu.VMEM((pieces, count, BLOCK // pieces, BLOCK), jnp.float32)],
        compiler_params=SMALL,
    )(vectors(left), vectors(right))


def my_half(first=0):
    half = BLOCK // 2
    return pl.ds(pl.multiple_of(((lax.axis_index("seq") & 1) ^ first) * half, half), half)


def far_kernel(left, arrived, kept, sent, whole):
    for j in range(arrived.shape[0]):
        whole[j] = lax.dot_general(
            left[j], arrived[j], (((0,), (0,)), ((), ())), preferred_element_type=jnp.float32
        )
    kept[...] = whole[:, my_half()]
    sent[...] = whole[:, my_half(1)].astype(jnp.bfloat16)


def far_products(left, arrived):
    count = arrived.shape[0]
    half = (count, BLOCK // 2, BLOCK)
    return pl.pallas_call(
        far_kernel,
        out_shape=[pltpu.VMEM(half, jnp.float32), pltpu.VMEM(half, jnp.bfloat16)],
        in_specs=[VMEM, VMEM],
        out_specs=[VMEM, VMEM],
        scratch_shapes=[pltpu.VMEM((count, BLOCK, BLOCK), jnp.float32)],
        name="far_products",
        compiler_params=SMALL,
    )(vectors(left), vectors(arrived))


def share_kernel(kept, received, still, sent):
    total = kept[...] + received[...].astype(jnp.float32)
    still[...] = total
    sent[...] = total.astype(jnp.bfloat16)


def share(kept, received):
    return pl.pallas_call(
        share_kernel,
        out_shape=[pltpu.VMEM(kept.shape, jnp.float32), pltpu.VMEM(kept.shape, jnp.bfloat16)],
        in_specs=[VMEM, VMEM],
        out_specs=[VMEM, VMEM],
        compiler_params=SMALL,
    )(vectors(kept), vectors(received))


def share_last_kernel(kept, received, sent):
    sent[...] = (kept[...] + received[...].astype(jnp.float32)).astype(jnp.bfloat16)


def share_last(kept, received):
    return pl.pallas_call(
        share_last_kernel,
        out_shape=pltpu.VMEM(kept.shape, jnp.bfloat16),
        in_specs=[VMEM, VMEM],
        out_specs=VMEM,
        compiler_params=SMALL,
    )(vectors(kept), vectors(received))


def compose_kernel(delivered, mine, other, owned, out):
    far_items, rows = mine.shape[0], BLOCK // 2
    for slot in range(out.shape[0]):
        out[slot] = delivered[:, slot].reshape(BLOCK, BLOCK)
        for half, source in ((my_half(), mine), (my_half(1), other)):
            value = out[slot, half].astype(jnp.float32)
            for j in range(far_items):
                flag = jnp.concatenate([owned[slot * far_items + j]] * (rows // 8))
                value = jnp.where(flag > 0, source[j].astype(jnp.float32), value)
            out[slot, half] = value.astype(jnp.bfloat16)


def compose(delivered, mine, other, owned):
    return pl.pallas_call(
        compose_kernel,
        out_shape=jax.ShapeDtypeStruct((delivered.shape[1], BLOCK, BLOCK), jnp.bfloat16),
        in_specs=[VMEM] * 4,
        out_specs=VMEM,
        name="compose",
        compiler_params=SMALL,
    )(vectors(delivered), vectors(mine), vectors(other), vectors(owned))


def plan_kernel(cols_per, per_peer, cols, owners, places, seen):
    me = lax.axis_index("tensor")
    for index in range(4):
        seen[index] = 0
    listed = range(cols.shape[1])
    distances = [lax.shift_right_logical(cols[0, k], cols_per.bit_length() - 1) ^ me for k in listed]
    placed_at = [owners[0, k] for k in listed]
    slot = jnp.int32(0)
    for k in listed:
        rank = jnp.minimum(seen[distances[k]], per_peer - 1)
        seen[distances[k]] = rank + 1
        slot = jnp.where(placed_at[k] == placed_at[k - 1], slot + 1, 0) if k else slot
        places[distances[k] * per_peer + rank] = placed_at[k] * CAP + jnp.minimum(slot, CAP - 1)


def plan(cols, owners, cols_per, per_peer):
    return pl.pallas_call(
        functools.partial(plan_kernel, cols_per, per_peer),
        out_shape=pltpu.SMEM((cols.shape[1],), jnp.int32),
        in_specs=[SMEM, SMEM],
        out_specs=SMEM,
        scratch_shapes=[pltpu.SMEM((4,), jnp.int32)],
        name="plan",
        compiler_params=SMALL,
    )(scalars(cols), scalars(owners))


def flag_kernel(per_peer, places, owned):
    first = lax.axis_index("seq") * CAP
    owned[...] = jnp.zeros_like(owned)
    for rank in range(per_peer):
        slot = places[3 * per_peer + rank] - first
        mine = jnp.logical_and(slot >= 0, slot < CAP)
        owned[jnp.where(mine, slot * per_peer + rank, CAP * per_peer)] = jnp.ones(owned.shape[1:], jnp.float32)


def flag_owned(places, per_peer):
    return pl.pallas_call(
        functools.partial(flag_kernel, per_peer),
        out_shape=pltpu.VMEM((CAP * per_peer + 1, 8, BLOCK), jnp.float32),
        in_specs=[SMEM],
        out_specs=VMEM,
        name="flag_owned",
        compiler_params=SMALL,
    )(scalars(places))


def settle_kernel(places, own, core, guests, out):
    out[...] = jnp.zeros_like(out)
    first = 0
    for source in (own, core, guests):
        for j in range(source.shape[0]):
            place = places[first + j]
            out[lax.shift_right_logical(place, CAP.bit_length() - 1), place & (CAP - 1)] = source[j]
        first += source.shape[0]


def settle(places, own, core, guests, pieces):
    _, rows, _ = guests.shape
    return pl.pallas_call(
        settle_kernel,
        out_shape=pltpu.VMEM((pieces, CAP, rows, BLOCK), jnp.bfloat16),
        in_specs=[SMEM] + [VMEM] * 3,
        out_specs=VMEM,
        name="settle",
        compiler_params=SMALL,
    )(scalars(places), vectors(own), vectors(core), vectors(guests))


def sparse_on_device(hidden, grad_out, block_rows, block_cols, block_owner):
    tensor_count, seq_count = lax.axis_size("tensor"), lax.axis_size("seq")
    cols_per = grad_out.shape[1] // BLOCK
    per_peer = block_cols.shape[1] // tensor_count

    def to_peer(value, distance):
        return lax.ppermute(value, "tensor", [(i, i ^ distance) for i in range(tensor_count)])

    def exchange(sent, distance):
        return lax.ppermute(sent, "seq", [(i, i ^ distance) for i in range(seq_count)])

    def reduce_pieces(order, kept, sent, counts):
        for step, distance in enumerate(order):
            received = exchange(sent, distance)
            if step == len(order) - 1:
                return finish(kept, received, counts)
            kept, sent = halve([(kept, received)])

    near_order, guest_order = (2, 1, 4), (1, 2, 4)
    for_cross, for_core = push_blocks(block_rows, block_cols, hidden, cols_per, per_peer)
    list2 = to_peer(block_cols, 2)
    guests = to_peer(for_cross, 2)
    from_core = to_peer(for_core, 1)
    list1 = to_peer(block_cols, 1)
    near_kept, near_sent = near_products(
        block_rows, block_cols, list1, hidden, grad_out, from_core, per_peer, seq_count, near_order
    )
    list3 = to_peer(list2, 1)
    own_sum, core_sum = reduce_pieces(near_order, near_kept, near_sent, (per_peer, per_peer))
    core_back = to_peer(core_sum, 1)
    for_far, for_guests, hidden_far = pack_blocks(block_rows, block_cols, list2, list3, hidden, grad_out, per_peer)
    from_far = to_peer(for_far, 3)
    places = plan(block_cols, block_owner, cols_per, per_peer)
    owned = flag_owned(places, per_peer)
    guest_kept, guest_sent = cross_products(guests, for_guests, seq_count, guest_order)
    (guest_sum,) = reduce_pieces(guest_order, guest_kept, guest_sent, (per_peer,))
    guest_back = to_peer(guest_sum, 2)
    kept, sent = far_products(hidden_far, from_far)
    for distance in guest_order:
        received = exchange(sent, distance)
        if distance == guest_order[-1]:
            sent = share_last(kept, received)
        else:
            kept, sent = share(kept, received)
    other = lax.ppermute(sent, "seq", [(i, i ^ 1) for i in range(seq_count)])
    placed = settle(places, own_sum, core_back, guest_back, seq_count)
    delivered = lax.all_to_all(placed, "seq", split_axis=0, concat_axis=0, tiled=True)
    return compose(delivered, sent, other, owned)[None]


def solution(mesh):
    tensor_count, seq_count = mesh.shape["tensor"], mesh.shape["seq"]
    placed = (
        P("seq", "tensor"),
        P("seq", "tensor"),
        P("tensor", None),
        P("tensor", None),
        P("tensor", None),
    )

    def on_device(hidden, grad_out, block_rows, block_cols, block_owner):
        listed = block_cols.shape[1]
        each_named_once = listed == 24 and tensor_count == 4
        whole_tiles = BLOCK % (seq_count * ROW_TILE) == 0
        step = sparse_on_device if each_named_once and whole_tiles else dense_on_device
        return step(hidden, grad_out, block_rows, block_cols, block_owner)

    return jax.shard_map(
        on_device,
        mesh=mesh,
        in_specs=placed,
        out_specs=P("tensor", "seq", None, None),
        check_vma=False,
    )
```

```python
import functools

import jax
import jax.numpy as jnp
from jax import lax
from jax.experimental import pallas as pl
from jax.experimental.pallas import tpu as pltpu
from jax.sharding import PartitionSpec as P


BLOCK = 128
CAP = 8
ROW_TILE = 16

SMEM = pl.BlockSpec(memory_space=pltpu.SMEM)
HBM = pl.BlockSpec(memory_space=pltpu.HBM)
SMALL = pltpu.CompilerParams(vmem_limit_bytes=8 << 20)
VMEM = pl.BlockSpec(memory_space=pltpu.VMEM)


def pick_slots(summed, starts, counts):
    slot_ids = starts[:, None] + jnp.arange(CAP, dtype=jnp.int32)[None, :]
    is_live = jnp.arange(CAP, dtype=jnp.int32)[None, :] < counts[:, None]
    picked = jnp.take(summed, jnp.minimum(slot_ids, summed.shape[0] - 1).reshape(-1), axis=0)
    picked = picked.reshape(slot_ids.shape[0], CAP, BLOCK, BLOCK)
    return jnp.where(is_live[:, :, None, None], picked, jnp.zeros_like(picked))


def dense_on_device(hidden, grad_out, block_rows, block_cols, block_owner):
    tok_rows = hidden.shape[0]
    hidden_sel = jnp.take(hidden.reshape(tok_rows, -1, BLOCK), block_rows[0], axis=1)
    cotangent = lax.all_gather(grad_out, "tensor", axis=1, tiled=True)
    grad_sel = jnp.take(cotangent.reshape(tok_rows, -1, BLOCK), block_cols[0], axis=1)
    partial_value = jnp.einsum(
        "tkr,tkc->krc", hidden_sel, grad_sel, preferred_element_type=jnp.float32
    ).astype(jnp.bfloat16)
    seq_count = lax.axis_size("seq")
    members = (block_owner[0][None, :] == jnp.arange(seq_count, dtype=jnp.int32)[:, None]).astype(jnp.int32)
    counts = jnp.sum(members, axis=1)
    starts = jnp.cumsum(counts) - counts
    outgoing = pick_slots(partial_value, starts, counts)
    received = lax.all_to_all(outgoing, "seq", split_axis=0, concat_axis=0, tiled=True)
    return jnp.sum(received, axis=0, dtype=jnp.float32).astype(jnp.bfloat16)[None]


def scalars(value):
    return pltpu.with_memory_space_constraint(value, pltpu.SMEM)


def in_hbm(value):
    return pltpu.with_memory_space_constraint(value, pltpu.HBM)


def vectors(value):
    return pltpu.with_memory_space_constraint(value, pltpu.VMEM)


def column(ref, index):
    return ref.at[:, pl.ds(pl.multiple_of(index * BLOCK, BLOCK), BLOCK)]


def listed_at(table, cols, values, owner, cols_per, per_peer):
    listed = [cols[0, k] - owner * cols_per for k in range(cols.shape[1])]
    taken = listed if values is None else [values[0, k] for k in range(cols.shape[1])]
    found = jnp.int32(0)
    for local, value in zip(listed, taken):
        hit = jnp.logical_and(local >= 0, local < cols_per)
        table[jnp.where(hit, jnp.minimum(found, per_peer - 1), per_peer)] = value
        found += hit.astype(jnp.int32)


def multiply(left, right):
    return lax.dot_general(left, right, (((0,), (0,)), ((), ())), preferred_element_type=jnp.float32)


def my_half(other=0):
    half = BLOCK // 2
    return pl.ds(pl.multiple_of(((lax.axis_index("seq") & 1) ^ other) * half, half), half)


def split_rows(whole, kept, sent):
    kept[...] = whole[:, my_half()]
    sent[...] = whole[:, my_half(1)].astype(jnp.bfloat16)


def row_halves(items):
    shape = (items, BLOCK // 2, BLOCK)
    return [pltpu.VMEM(shape, jnp.float32), pltpu.VMEM(shape, jnp.bfloat16)]


def fetch(pairs, sems):
    copies = [pltpu.make_async_copy(source, there, sems.at[n]) for n, (source, there) in enumerate(pairs)]
    for copy in copies:
        copy.start()
    return copies


def start_columns(source, table, there, sems):
    copies = [pltpu.make_async_copy(column(source, table[j]), there.at[j], sems.at[j]) for j in range(there.shape[0])]
    for copy in copies:
        copy.start()
    return copies


def push_kernel(cols_per, per_peer, all_rows, all_cols, hidden, cross, core, rows, cols, table, list_sems, sems):
    for copy in fetch(((all_rows, rows), (all_cols, cols)), list_sems):
        copy.wait()
    me = lax.axis_index("tensor")
    copies = []
    for n, (distance, there) in enumerate(((2, cross), (1, core))):
        listed_at(table, cols, rows, me ^ distance, cols_per, per_peer)
        copies += start_columns(hidden, table, there, sems.at[n])
    for copy in copies:
        copy.wait()


def push_blocks(rows, cols, hidden, cols_per, per_peer):
    return pl.pallas_call(
        functools.partial(push_kernel, cols_per, per_peer),
        out_shape=[pltpu.VMEM((per_peer, hidden.shape[0], BLOCK), hidden.dtype)] * 2,
        in_specs=[HBM, HBM, HBM],
        out_specs=[VMEM, VMEM],
        scratch_shapes=[
            pltpu.SMEM(rows.shape, jnp.int32),
            pltpu.SMEM(cols.shape, jnp.int32),
            pltpu.SMEM((per_peer + 1,), jnp.int32),
            pltpu.SemaphoreType.DMA((2,)),
            pltpu.SemaphoreType.DMA((2, per_peer)),
        ],
        name="push_blocks",
        compiler_params=SMALL,
    )(in_hbm(rows), in_hbm(cols), in_hbm(hidden))


def near_kernel(cols_per, per_peer, all_rows, all_cols, came1, hidden, grad_out, arrived, kept, sent, own, right, whole, rows, cols, list1, table, list_sems, sems):
    me = lax.axis_index("tensor")
    for copy in fetch(((all_rows, rows), (all_cols, cols), (came1, list1)), list_sems):
        copy.wait()
    listed_at(table, cols, rows, me, cols_per, per_peer)
    copies = start_columns(hidden, table, own, sems.at[0])
    listed_at(table, cols, None, me, cols_per, per_peer)
    copies += start_columns(grad_out, table, right.at[pl.ds(0, per_peer)], sems.at[1])
    listed_at(table, list1, None, me, cols_per, per_peer)
    copies += start_columns(grad_out, table, right.at[pl.ds(per_peer, per_peer)], sems.at[2])
    for copy in copies:
        copy.wait()
    for item in range(2 * per_peer):
        left = own[item] if item < per_peer else arrived[item - per_peer]
        whole[item] = multiply(left, right[item])
    split_rows(whole, kept, sent)


def near_products(rows, cols, list1, hidden, grad_out, arrived, per_peer):
    tok_rows, width = grad_out.shape
    return pl.pallas_call(
        functools.partial(near_kernel, width // BLOCK, per_peer),
        out_shape=row_halves(2 * per_peer),
        in_specs=[HBM, HBM, VMEM, HBM, HBM, VMEM],
        out_specs=[VMEM, VMEM],
        scratch_shapes=[
            pltpu.VMEM((per_peer, tok_rows, BLOCK), jnp.bfloat16),
            pltpu.VMEM((2 * per_peer, tok_rows, BLOCK), jnp.bfloat16),
            pltpu.VMEM((2 * per_peer, BLOCK, BLOCK), jnp.float32),
            pltpu.SMEM(rows.shape, jnp.int32),
            pltpu.SMEM(cols.shape, jnp.int32),
            pltpu.SMEM(list1.shape, jnp.int32),
            pltpu.SMEM((per_peer + 1,), jnp.int32),
            pltpu.SemaphoreType.DMA((3,)),
            pltpu.SemaphoreType.DMA((3, per_peer)),
        ],
        name="near_products",
        compiler_params=SMALL,
    )(in_hbm(rows), in_hbm(cols), vectors(list1), in_hbm(hidden), in_hbm(grad_out), vectors(arrived))


def pack_kernel(cols_per, per_peer, all_rows, all_cols, came2, came3, hidden, grad_out, for_far, for_guests, hidden_far, rows, cols, list2, list3, table, list_sems, sems):
    me = lax.axis_index("tensor")
    for copy in fetch(((all_rows, rows), (all_cols, cols), (came2, list2), (came3, list3)), list_sems):
        copy.wait()
    listed_at(table, list3, None, me, cols_per, per_peer)
    copies = start_columns(grad_out, table, for_far, sems.at[0])
    listed_at(table, list2, None, me, cols_per, per_peer)
    copies += start_columns(grad_out, table, for_guests, sems.at[1])
    listed_at(table, cols, rows, me ^ 3, cols_per, per_peer)
    copies += start_columns(hidden, table, hidden_far, sems.at[2])
    for copy in copies:
        copy.wait()


def pack_blocks(rows, cols, list2, list3, hidden, grad_out, per_peer):
    tok_rows, width = grad_out.shape
    return pl.pallas_call(
        functools.partial(pack_kernel, width // BLOCK, per_peer),
        out_shape=[pltpu.VMEM((per_peer, tok_rows, BLOCK), grad_out.dtype)] * 3,
        in_specs=[HBM, HBM, VMEM, VMEM, HBM, HBM],
        out_specs=[VMEM, VMEM, VMEM],
        scratch_shapes=[pltpu.SMEM(value.shape, jnp.int32) for value in (rows, cols, list2, list3)]
        + [
            pltpu.SMEM((per_peer + 1,), jnp.int32),
            pltpu.SemaphoreType.DMA((4,)),
            pltpu.SemaphoreType.DMA((3, per_peer)),
        ],
        name="pack_blocks",
        compiler_params=SMALL,
    )(in_hbm(rows), in_hbm(cols), vectors(list2), vectors(list3), in_hbm(hidden), in_hbm(grad_out))


def cross_kernel(left, right, kept, sent, whole):
    for j in range(left.shape[0]):
        whole[j] = multiply(left[j], right[j])
    split_rows(whole, kept, sent)


def cross_products(left, right):
    count = left.shape[0]
    return pl.pallas_call(
        cross_kernel,
        out_shape=row_halves(count),
        in_specs=[VMEM, VMEM],
        out_specs=[VMEM, VMEM],
        scratch_shapes=[pltpu.VMEM((count, BLOCK, BLOCK), jnp.float32)],
        compiler_params=SMALL,
    )(vectors(left), vectors(right))


def my_quarter(other=0):
    quarter = BLOCK // 4
    bit = lax.shift_right_logical(lax.axis_index("seq"), 1) & 1
    return pl.ds(pl.multiple_of((bit ^ other) * quarter, quarter), quarter)


def quarter_kernel(kept, received, still, sent):
    still[...] = kept[:, my_quarter()] + received[:, my_quarter()].astype(jnp.float32)
    total = kept[:, my_quarter(1)] + received[:, my_quarter(1)].astype(jnp.float32)
    sent[...] = total.astype(jnp.bfloat16)


def quarter(kept, received):
    shape = (kept.shape[0], BLOCK // 4, BLOCK)
    return pl.pallas_call(
        quarter_kernel,
        out_shape=[pltpu.VMEM(shape, jnp.float32), pltpu.VMEM(shape, jnp.bfloat16)],
        in_specs=[VMEM, VMEM],
        out_specs=[VMEM, VMEM],
        compiler_params=SMALL,
    )(vectors(kept), vectors(received))


def join_kernel(mine, other, *outs):
    first = 0
    for out in outs:
        items = pl.ds(first, out.shape[0])
        out[:, my_quarter()] = mine[items]
        out[:, my_quarter(1)] = other[items]
        first += out.shape[0]


def join(mine, other, counts):
    return pl.pallas_call(
        join_kernel,
        out_shape=[pltpu.VMEM((count, BLOCK // 2, BLOCK), jnp.bfloat16) for count in counts],
        in_specs=[VMEM, VMEM],
        out_specs=[VMEM] * len(counts),
        compiler_params=SMALL,
    )(vectors(mine), vectors(other))


def share_kernel(kept, received, still, sent):
    total = kept[...] + received[...].astype(jnp.float32)
    still[...] = total
    sent[...] = total.astype(jnp.bfloat16)


def share(kept, received):
    return pl.pallas_call(
        share_kernel,
        out_shape=[pltpu.VMEM(kept.shape, jnp.float32), pltpu.VMEM(kept.shape, jnp.bfloat16)],
        in_specs=[VMEM, VMEM],
        out_specs=[VMEM, VMEM],
        compiler_params=SMALL,
    )(vectors(kept), vectors(received))


def finish_kernel(kept, received, *outs):
    first = 0
    for out in outs:
        items = pl.ds(first, out.shape[0])
        out[...] = (kept[items] + received[items].astype(jnp.float32)).astype(jnp.bfloat16)
        first += out.shape[0]


def finish(kept, received, counts):
    return pl.pallas_call(
        finish_kernel,
        out_shape=[pltpu.VMEM((count,) + kept.shape[1:], jnp.bfloat16) for count in counts],
        in_specs=[VMEM, VMEM],
        out_specs=[VMEM] * len(counts),
        compiler_params=SMALL,
    )(vectors(kept), vectors(received))


def plan_kernel(cols_per, per_peer, cols, owners, places, seen):
    me = lax.axis_index("tensor")
    for index in range(4):
        seen[index] = 0
    listed = range(cols.shape[1])
    distances = [lax.shift_right_logical(cols[0, k], cols_per.bit_length() - 1) ^ me for k in listed]
    placed_at = [owners[0, k] for k in listed]
    slot = jnp.int32(0)
    for k in listed:
        rank = jnp.minimum(seen[distances[k]], per_peer - 1)
        seen[distances[k]] = rank + 1
        slot = jnp.where(placed_at[k] == placed_at[k - 1], slot + 1, 0) if k else slot
        places[distances[k] * per_peer + rank] = placed_at[k] * CAP + jnp.minimum(slot, CAP - 1)


def plan(cols, owners, cols_per, per_peer):
    return pl.pallas_call(
        functools.partial(plan_kernel, cols_per, per_peer),
        out_shape=pltpu.SMEM((cols.shape[1],), jnp.int32),
        in_specs=[SMEM, SMEM],
        out_specs=SMEM,
        scratch_shapes=[pltpu.SMEM((4,), jnp.int32)],
        name="plan",
        compiler_params=SMALL,
    )(scalars(cols), scalars(owners))


def settle_kernel(places, own, core, guests, kept, received, mine, sent):
    me = lax.axis_index("seq")
    mine[...] = jnp.zeros_like(mine)
    sent[...] = jnp.zeros_like(sent)
    spare = mine.shape[0] - 1
    first = 0
    for source in (own, core, guests, None):
        for j in range(guests.shape[0]):
            place = places[first + j]
            owner, slot = lax.shift_right_logical(place, CAP.bit_length() - 1), place & (CAP - 1)
            if source is None:
                value = (kept[j] + received[j].astype(jnp.float32)).astype(jnp.bfloat16)
            else:
                value = source[j]
            mine[jnp.where(owner == me, slot, spare)] = value
            sent[jnp.where(owner == (me ^ 1), slot, spare)] = value
        first += guests.shape[0]


def settle(places, own, core, guests, kept, received):
    _, rows, _ = guests.shape
    return pl.pallas_call(
        settle_kernel,
        out_shape=[pltpu.VMEM((CAP + 1, rows, BLOCK), jnp.bfloat16)] * 2,
        in_specs=[SMEM] + [VMEM] * 5,
        out_specs=[VMEM, VMEM],
        name="settle",
        compiler_params=SMALL,
    )(scalars(places), vectors(own), vectors(core), vectors(guests), vectors(kept), vectors(received))


def compose_kernel(mine, other, out):
    for slot in range(out.shape[0]):
        out[slot, my_half()] = mine[slot]
        out[slot, my_half(1)] = other[slot]


def compose(mine, other):
    return pl.pallas_call(
        compose_kernel,
        out_shape=jax.ShapeDtypeStruct((CAP, BLOCK, BLOCK), jnp.bfloat16),
        in_specs=[VMEM, VMEM],
        out_specs=VMEM,
        name="compose",
        compiler_params=SMALL,
    )(vectors(mine), vectors(other))


def sparse_on_device(hidden, grad_out, block_rows, block_cols, block_owner):
    tensor_count, seq_count = lax.axis_size("tensor"), lax.axis_size("seq")
    cols_per = grad_out.shape[1] // BLOCK
    per_peer = block_cols.shape[1] // tensor_count

    def to_peer(value, distance):
        return lax.ppermute(value, "tensor", [(i, i ^ distance) for i in range(tensor_count)])

    def exchange(sent, distance):
        return lax.ppermute(sent, "seq", [(i, i ^ distance) for i in range(seq_count)])

    def sum_over_seq(order, kept, sent):
        for step, distance in enumerate(order):
            received = exchange(sent, distance)
            if step == len(order) - 1:
                return kept, received
            kept, sent = share(kept, received)

    cross_order = (1, 2, 4)
    for_cross, for_core = push_blocks(block_rows, block_cols, hidden, cols_per, per_peer)
    list2 = to_peer(block_cols, 2)
    guests = to_peer(for_cross, 2)
    from_core = to_peer(for_core, 1)
    list1 = to_peer(block_cols, 1)
    near_kept, near_sent = near_products(
        block_rows, block_cols, list1, hidden, grad_out, from_core, per_peer
    )
    list3 = to_peer(list2, 1)
    near_came = exchange(near_sent, 1)
    near_kept, near_sent = quarter(near_kept, near_came)
    near_came = exchange(near_sent, 2)
    near_kept, near_sent = share(near_kept, near_came)
    near_came = exchange(near_sent, 4)
    (near_mine,) = finish(near_kept, near_came, (2 * per_peer,))
    near_other = exchange(near_mine, 2)
    own_sum, core_sum = join(near_mine, near_other, (per_peer, per_peer))
    core_back = to_peer(core_sum, 1)
    for_far, for_guests, hidden_far = pack_blocks(block_rows, block_cols, list2, list3, hidden, grad_out, per_peer)
    from_far = to_peer(for_far, 3)
    places = plan(block_cols, block_owner, cols_per, per_peer)
    guest_kept, guest_sent = cross_products(guests, for_guests)
    guest_kept, guest_came = sum_over_seq(cross_order, guest_kept, guest_sent)
    (guest_sum,) = finish(guest_kept, guest_came, (per_peer,))
    guest_back = to_peer(guest_sum, 2)
    far_kept, far_sent = cross_products(hidden_far, from_far)
    far_kept, far_came = sum_over_seq(cross_order, far_kept, far_sent)
    mine, sent = settle(places, own_sum, core_back, guest_back, far_kept, far_came)
    other = exchange(sent, 1)
    return compose(mine, other)[None]


def solution(mesh):
    tensor_count, seq_count = mesh.shape["tensor"], mesh.shape["seq"]
    placed = (
        P("seq", "tensor"),
        P("seq", "tensor"),
        P("tensor", None),
        P("tensor", None),
        P("tensor", None),
    )

    def on_device(hidden, grad_out, block_rows, block_cols, block_owner):
        listed = block_cols.shape[1]
        each_named_once = listed == 24 and tensor_count == 4
        whole_tiles = BLOCK % (seq_count * ROW_TILE) == 0
        step = sparse_on_device if each_named_once and whole_tiles else dense_on_device
        return step(hidden, grad_out, block_rows, block_cols, block_owner)

    return jax.shard_map(
        on_device,
        mesh=mesh,
        in_specs=placed,
        out_specs=P("tensor", "seq", None, None),
        check_vma=False,
    )
```

```python
import functools

import jax
import jax.numpy as jnp
from jax import lax
from jax.experimental import pallas as pl
from jax.experimental.pallas import tpu as pltpu
from jax.sharding import PartitionSpec as P


BLOCK = 128
CAP = 8
ROW_TILE = 16

SMEM = pl.BlockSpec(memory_space=pltpu.SMEM)
HBM = pl.BlockSpec(memory_space=pltpu.HBM)
SMALL = pltpu.CompilerParams(vmem_limit_bytes=8 << 20)
VMEM = pl.BlockSpec(memory_space=pltpu.VMEM)


def pick_slots(summed, starts, counts):
    slot_ids = starts[:, None] + jnp.arange(CAP, dtype=jnp.int32)[None, :]
    is_live = jnp.arange(CAP, dtype=jnp.int32)[None, :] < counts[:, None]
    picked = jnp.take(summed, jnp.minimum(slot_ids, summed.shape[0] - 1).reshape(-1), axis=0)
    picked = picked.reshape(slot_ids.shape[0], CAP, BLOCK, BLOCK)
    return jnp.where(is_live[:, :, None, None], picked, jnp.zeros_like(picked))


def dense_on_device(hidden, grad_out, block_rows, block_cols, block_owner):
    tok_rows = hidden.shape[0]
    hidden_sel = jnp.take(hidden.reshape(tok_rows, -1, BLOCK), block_rows[0], axis=1)
    cotangent = lax.all_gather(grad_out, "tensor", axis=1, tiled=True)
    grad_sel = jnp.take(cotangent.reshape(tok_rows, -1, BLOCK), block_cols[0], axis=1)
    partial_value = jnp.einsum(
        "tkr,tkc->krc", hidden_sel, grad_sel, preferred_element_type=jnp.float32
    ).astype(jnp.bfloat16)
    seq_count = lax.axis_size("seq")
    members = (block_owner[0][None, :] == jnp.arange(seq_count, dtype=jnp.int32)[:, None]).astype(jnp.int32)
    counts = jnp.sum(members, axis=1)
    starts = jnp.cumsum(counts) - counts
    outgoing = pick_slots(partial_value, starts, counts)
    received = lax.all_to_all(outgoing, "seq", split_axis=0, concat_axis=0, tiled=True)
    return jnp.sum(received, axis=0, dtype=jnp.float32).astype(jnp.bfloat16)[None]


def scalars(value):
    return pltpu.with_memory_space_constraint(value, pltpu.SMEM)


def in_hbm(value):
    return pltpu.with_memory_space_constraint(value, pltpu.HBM)


def vectors(value):
    return pltpu.with_memory_space_constraint(value, pltpu.VMEM)


def column(ref, index):
    return ref.at[:, pl.ds(pl.multiple_of(index * BLOCK, BLOCK), BLOCK)]


def listed_at(table, cols, values, owner, cols_per, per_peer):
    listed = [cols[0, k] - owner * cols_per for k in range(cols.shape[1])]
    taken = listed if values is None else [values[0, k] for k in range(cols.shape[1])]
    found = jnp.int32(0)
    for local, value in zip(listed, taken):
        hit = jnp.logical_and(local >= 0, local < cols_per)
        table[jnp.where(hit, jnp.minimum(found, per_peer - 1), per_peer)] = value
        found += hit.astype(jnp.int32)


def multiply(left, right):
    return lax.dot_general(left, right, (((0,), (0,)), ((), ())), preferred_element_type=jnp.float32)


def my_half(other=0):
    half = BLOCK // 2
    return pl.ds(pl.multiple_of(((lax.axis_index("seq") & 1) ^ other) * half, half), half)


def split_rows(whole, kept, sent):
    kept[...] = whole[:, my_half()]
    sent[...] = whole[:, my_half(1)].astype(jnp.bfloat16)


def row_halves(items):
    shape = (items, BLOCK // 2, BLOCK)
    return [pltpu.VMEM(shape, jnp.float32), pltpu.VMEM(shape, jnp.bfloat16)]


def fetch(pairs, sems):
    copies = [pltpu.make_async_copy(source, there, sems.at[n]) for n, (source, there) in enumerate(pairs)]
    for copy in copies:
        copy.start()
    return copies


def start_columns(source, table, there, sems):
    copies = [pltpu.make_async_copy(column(source, table[j]), there.at[j], sems.at[j]) for j in range(there.shape[0])]
    for copy in copies:
        copy.start()
    return copies


def push_kernel(cols_per, per_peer, all_rows, all_cols, hidden, cross, core, rows, cols, table, list_sems, sems):
    for copy in fetch(((all_rows, rows), (all_cols, cols)), list_sems):
        copy.wait()
    me = lax.axis_index("tensor")
    copies = []
    for n, (distance, there) in enumerate(((2, cross), (1, core))):
        listed_at(table, cols, rows, me ^ distance, cols_per, per_peer)
        copies += start_columns(hidden, table, there, sems.at[n])
    for copy in copies:
        copy.wait()


def push_blocks(rows, cols, hidden, cols_per, per_peer):
    return pl.pallas_call(
        functools.partial(push_kernel, cols_per, per_peer),
        out_shape=[pltpu.VMEM((per_peer, hidden.shape[0], BLOCK), hidden.dtype)] * 2,
        in_specs=[HBM, HBM, HBM],
        out_specs=[VMEM, VMEM],
        scratch_shapes=[
            pltpu.SMEM(rows.shape, jnp.int32),
            pltpu.SMEM(cols.shape, jnp.int32),
            pltpu.SMEM((per_peer + 1,), jnp.int32),
            pltpu.SemaphoreType.DMA((2,)),
            pltpu.SemaphoreType.DMA((2, per_peer)),
        ],
        name="push_blocks",
        compiler_params=SMALL,
    )(in_hbm(rows), in_hbm(cols), in_hbm(hidden))


def near_kernel(cols_per, per_peer, all_rows, all_cols, came1, hidden, grad_out, arrived, kept, sent, own, right, whole, rows, cols, list1, table, list_sems, sems):
    me = lax.axis_index("tensor")
    for copy in fetch(((all_rows, rows), (all_cols, cols), (came1, list1)), list_sems):
        copy.wait()
    listed_at(table, cols, rows, me, cols_per, per_peer)
    copies = start_columns(hidden, table, own, sems.at[0])
    listed_at(table, cols, None, me, cols_per, per_peer)
    copies += start_columns(grad_out, table, right.at[pl.ds(0, per_peer)], sems.at[1])
    listed_at(table, list1, None, me, cols_per, per_peer)
    copies += start_columns(grad_out, table, right.at[pl.ds(per_peer, per_peer)], sems.at[2])
    for copy in copies:
        copy.wait()
    for item in range(2 * per_peer):
        left = own[item] if item < per_peer else arrived[item - per_peer]
        whole[item] = multiply(left, right[item])
    split_rows(whole, kept, sent)


def near_products(rows, cols, list1, hidden, grad_out, arrived, per_peer):
    tok_rows, width = grad_out.shape
    return pl.pallas_call(
        functools.partial(near_kernel, width // BLOCK, per_peer),
        out_shape=row_halves(2 * per_peer),
        in_specs=[HBM, HBM, VMEM, HBM, HBM, VMEM],
        out_specs=[VMEM, VMEM],
        scratch_shapes=[
            pltpu.VMEM((per_peer, tok_rows, BLOCK), jnp.bfloat16),
            pltpu.VMEM((2 * per_peer, tok_rows, BLOCK), jnp.bfloat16),
            pltpu.VMEM((2 * per_peer, BLOCK, BLOCK), jnp.float32),
            pltpu.SMEM(rows.shape, jnp.int32),
            pltpu.SMEM(cols.shape, jnp.int32),
            pltpu.SMEM(list1.shape, jnp.int32),
            pltpu.SMEM((per_peer + 1,), jnp.int32),
            pltpu.SemaphoreType.DMA((3,)),
            pltpu.SemaphoreType.DMA((3, per_peer)),
        ],
        name="near_products",
        compiler_params=SMALL,
    )(in_hbm(rows), in_hbm(cols), vectors(list1), in_hbm(hidden), in_hbm(grad_out), vectors(arrived))


def pack_kernel(cols_per, per_peer, all_rows, all_cols, came2, came3, hidden, grad_out, for_far, for_guests, hidden_far, rows, cols, list2, list3, table, list_sems, sems):
    me = lax.axis_index("tensor")
    for copy in fetch(((all_rows, rows), (all_cols, cols), (came2, list2), (came3, list3)), list_sems):
        copy.wait()
    listed_at(table, list3, None, me, cols_per, per_peer)
    copies = start_columns(grad_out, table, for_far, sems.at[0])
    listed_at(table, list2, None, me, cols_per, per_peer)
    copies += start_columns(grad_out, table, for_guests, sems.at[1])
    listed_at(table, cols, rows, me ^ 3, cols_per, per_peer)
    copies += start_columns(hidden, table, hidden_far, sems.at[2])
    for copy in copies:
        copy.wait()


def pack_blocks(rows, cols, list2, list3, hidden, grad_out, per_peer):
    tok_rows, width = grad_out.shape
    return pl.pallas_call(
        functools.partial(pack_kernel, width // BLOCK, per_peer),
        out_shape=[pltpu.VMEM((per_peer, tok_rows, BLOCK), grad_out.dtype)] * 3,
        in_specs=[HBM, HBM, VMEM, VMEM, HBM, HBM],
        out_specs=[VMEM, VMEM, VMEM],
        scratch_shapes=[pltpu.SMEM(value.shape, jnp.int32) for value in (rows, cols, list2, list3)]
        + [
            pltpu.SMEM((per_peer + 1,), jnp.int32),
            pltpu.SemaphoreType.DMA((4,)),
            pltpu.SemaphoreType.DMA((3, per_peer)),
        ],
        name="pack_blocks",
        compiler_params=SMALL,
    )(in_hbm(rows), in_hbm(cols), vectors(list2), vectors(list3), in_hbm(hidden), in_hbm(grad_out))


def cross_kernel(left, right, kept, sent, whole):
    for j in range(left.shape[0]):
        whole[j] = multiply(left[j], right[j])
    split_rows(whole, kept, sent)


def cross_products(left, right):
    count = left.shape[0]
    return pl.pallas_call(
        cross_kernel,
        out_shape=row_halves(count),
        in_specs=[VMEM, VMEM],
        out_specs=[VMEM, VMEM],
        scratch_shapes=[pltpu.VMEM((count, BLOCK, BLOCK), jnp.float32)],
        compiler_params=SMALL,
    )(vectors(left), vectors(right))


def my_quarter(other=0):
    quarter = BLOCK // 4
    bit = lax.shift_right_logical(lax.axis_index("seq"), 1) & 1
    return pl.ds(pl.multiple_of((bit ^ other) * quarter, quarter), quarter)


def quarter_kernel(kept, received, still, sent):
    still[...] = kept[:, my_quarter()] + received[:, my_quarter()].astype(jnp.float32)
    total = kept[:, my_quarter(1)] + received[:, my_quarter(1)].astype(jnp.float32)
    sent[...] = total.astype(jnp.bfloat16)


def quarter(kept, received):
    shape = (kept.shape[0], BLOCK // 4, BLOCK)
    return pl.pallas_call(
        quarter_kernel,
        out_shape=[pltpu.VMEM(shape, jnp.float32), pltpu.VMEM(shape, jnp.bfloat16)],
        in_specs=[VMEM, VMEM],
        out_specs=[VMEM, VMEM],
        compiler_params=SMALL,
    )(vectors(kept), vectors(received))


def join_kernel(mine, other, *outs):
    first = 0
    for out in outs:
        items = pl.ds(first, out.shape[0])
        out[:, my_quarter()] = mine[items]
        out[:, my_quarter(1)] = other[items]
        first += out.shape[0]


def join(mine, other, counts):
    return pl.pallas_call(
        join_kernel,
        out_shape=[pltpu.VMEM((count, BLOCK // 2, BLOCK), jnp.bfloat16) for count in counts],
        in_specs=[VMEM, VMEM],
        out_specs=[VMEM] * len(counts),
        compiler_params=SMALL,
    )(vectors(mine), vectors(other))


def share_kernel(kept, received, still, sent):
    total = kept[...] + received[...].astype(jnp.float32)
    still[...] = total
    sent[...] = total.astype(jnp.bfloat16)


def share(kept, received):
    return pl.pallas_call(
        share_kernel,
        out_shape=[pltpu.VMEM(kept.shape, jnp.float32), pltpu.VMEM(kept.shape, jnp.bfloat16)],
        in_specs=[VMEM, VMEM],
        out_specs=[VMEM, VMEM],
        compiler_params=SMALL,
    )(vectors(kept), vectors(received))


def finish_kernel(kept, received, *outs):
    first = 0
    for out in outs:
        items = pl.ds(first, out.shape[0])
        out[...] = (kept[items] + received[items].astype(jnp.float32)).astype(jnp.bfloat16)
        first += out.shape[0]


def finish(kept, received, counts):
    return pl.pallas_call(
        finish_kernel,
        out_shape=[pltpu.VMEM((count,) + kept.shape[1:], jnp.bfloat16) for count in counts],
        in_specs=[VMEM, VMEM],
        out_specs=[VMEM] * len(counts),
        compiler_params=SMALL,
    )(vectors(kept), vectors(received))


def plan_kernel(cols_per, per_peer, cols, owners, places, seen):
    me = lax.axis_index("tensor")
    for index in range(4):
        seen[index] = 0
    listed = range(cols.shape[1])
    distances = [lax.shift_right_logical(cols[0, k], cols_per.bit_length() - 1) ^ me for k in listed]
    placed_at = [owners[0, k] for k in listed]
    slot = jnp.int32(0)
    for k in listed:
        rank = jnp.minimum(seen[distances[k]], per_peer - 1)
        seen[distances[k]] = rank + 1
        slot = jnp.where(placed_at[k] == placed_at[k - 1], slot + 1, 0) if k else slot
        places[distances[k] * per_peer + rank] = placed_at[k] * CAP + jnp.minimum(slot, CAP - 1)


def plan(cols, owners, cols_per, per_peer):
    return pl.pallas_call(
        functools.partial(plan_kernel, cols_per, per_peer),
        out_shape=pltpu.SMEM((cols.shape[1],), jnp.int32),
        in_specs=[SMEM, SMEM],
        out_specs=SMEM,
        scratch_shapes=[pltpu.SMEM((4,), jnp.int32)],
        name="plan",
        compiler_params=SMALL,
    )(scalars(cols), scalars(owners))


def settle_kernel(places, own, core, guests, kept, received, mine, sent, theirs):
    me = lax.axis_index("seq")
    mine[...] = jnp.zeros_like(mine)
    theirs[...] = jnp.zeros_like(theirs)
    spare = mine.shape[0] - 1
    first = 0
    for source in (own, core, guests, None):
        for j in range(guests.shape[0]):
            place = places[first + j]
            owner, slot = lax.shift_right_logical(place, CAP.bit_length() - 1), place & (CAP - 1)
            if source is None:
                value = (kept[j] + received[j].astype(jnp.float32)).astype(jnp.bfloat16)
            else:
                value = source[j]
            mine[jnp.where(owner == me, slot, spare)] = value
            theirs[jnp.where(owner == (me ^ 1), slot, spare)] = value
        first += guests.shape[0]
    sent[...] = theirs[:spare]


def settle(places, own, core, guests, kept, received):
    _, rows, _ = guests.shape
    slots = [(CAP + 1, rows, BLOCK), (CAP, rows, BLOCK)]
    return pl.pallas_call(
        settle_kernel,
        out_shape=[pltpu.VMEM(shape, jnp.bfloat16) for shape in slots],
        in_specs=[SMEM] + [VMEM] * 5,
        out_specs=[VMEM, VMEM],
        scratch_shapes=[pltpu.VMEM(slots[0], jnp.bfloat16)],
        name="settle",
        compiler_params=SMALL,
    )(scalars(places), vectors(own), vectors(core), vectors(guests), vectors(kept), vectors(received))


def compose_kernel(mine, other, out):
    for slot in range(out.shape[0]):
        out[slot, my_half()] = mine[slot]
        out[slot, my_half(1)] = other[slot]


def compose(mine, other):
    return pl.pallas_call(
        compose_kernel,
        out_shape=jax.ShapeDtypeStruct((CAP, BLOCK, BLOCK), jnp.bfloat16),
        in_specs=[VMEM, VMEM],
        out_specs=VMEM,
        name="compose",
        compiler_params=SMALL,
    )(vectors(mine), vectors(other))


def sparse_on_device(hidden, grad_out, block_rows, block_cols, block_owner):
    tensor_count, seq_count = lax.axis_size("tensor"), lax.axis_size("seq")
    cols_per = grad_out.shape[1] // BLOCK
    per_peer = block_cols.shape[1] // tensor_count

    def to_peer(value, distance):
        return lax.ppermute(value, "tensor", [(i, i ^ distance) for i in range(tensor_count)])

    def exchange(sent, distance):
        return lax.ppermute(sent, "seq", [(i, i ^ distance) for i in range(seq_count)])

    def sum_over_seq(order, kept, sent):
        for step, distance in enumerate(order):
            received = exchange(sent, distance)
            if step == len(order) - 1:
                return kept, received
            kept, sent = share(kept, received)

    cross_order = (1, 2, 4)
    for_cross, for_core = push_blocks(block_rows, block_cols, hidden, cols_per, per_peer)
    list2 = to_peer(block_cols, 2)
    guests = to_peer(for_cross, 2)
    from_core = to_peer(for_core, 1)
    list1 = to_peer(block_cols, 1)
    near_kept, near_sent = near_products(
        block_rows, block_cols, list1, hidden, grad_out, from_core, per_peer
    )
    list3 = to_peer(list2, 1)
    near_came = exchange(near_sent, 1)
    near_kept, near_sent = quarter(near_kept, near_came)
    near_came = exchange(near_sent, 2)
    near_kept, near_sent = share(near_kept, near_came)
    near_came = exchange(near_sent, 4)
    (near_mine,) = finish(near_kept, near_came, (2 * per_peer,))
    near_other = exchange(near_mine, 2)
    own_sum, core_sum = join(near_mine, near_other, (per_peer, per_peer))
    core_back = to_peer(core_sum, 1)
    for_far, for_guests, hidden_far = pack_blocks(block_rows, block_cols, list2, list3, hidden, grad_out, per_peer)
    from_far = to_peer(for_far, 3)
    places = plan(block_cols, block_owner, cols_per, per_peer)
    guest_kept, guest_sent = cross_products(guests, for_guests)
    guest_kept, guest_came = sum_over_seq(cross_order, guest_kept, guest_sent)
    (guest_sum,) = finish(guest_kept, guest_came, (per_peer,))
    guest_back = to_peer(guest_sum, 2)
    far_kept, far_sent = cross_products(hidden_far, from_far)
    far_kept, far_came = sum_over_seq(cross_order, far_kept, far_sent)
    mine, sent = settle(places, own_sum, core_back, guest_back, far_kept, far_came)
    other = exchange(sent, 1)
    return compose(mine, other)[None]


def solution(mesh):
    tensor_count, seq_count = mesh.shape["tensor"], mesh.shape["seq"]
    placed = (
        P("seq", "tensor"),
        P("seq", "tensor"),
        P("tensor", None),
        P("tensor", None),
        P("tensor", None),
    )

    def on_device(hidden, grad_out, block_rows, block_cols, block_owner):
        listed = block_cols.shape[1]
        each_named_once = listed == 24 and tensor_count == 4
        whole_tiles = BLOCK % (seq_count * ROW_TILE) == 0
        step = sparse_on_device if each_named_once and whole_tiles else dense_on_device
        return step(hidden, grad_out, block_rows, block_cols, block_owner)

    return jax.shard_map(
        on_device,
        mesh=mesh,
        in_specs=placed,
        out_specs=P("tensor", "seq", None, None),
        check_vma=False,
    )
```
